512 devices in a mesh: row: 32 (over z, core), col: 16 (over y, x).
Axes of the slice: x: 4, y: 4, z: 16, core: 2. Of those that a mesh axis runs over, the one named last changes fastest.
Arguments:
- train_points: float32 [64, 32768], P(None, ('row', 'col')), may hold values from -6 to 6
- cand_points: float32 [64, 32768], P(None, ('row', 'col')), may hold values from -6 to 6
- inv_length: float32 [64], replicated, may hold values from 0.04 to 0.7
- noise: float32 [32768], P(('row', 'col')), may hold values from 0.5 to 4
- targets: float32 [16, 32768], P(None, ('row', 'col')), may hold values from -15 to 15
Outputs:
- solution: float32 [16, 32768], P(None, ('row', 'col'))
- post_mean: float32 [16, 32768], P(None, ('row', 'col'))
The draws below stay inside these ranges and needn't reach their ends.
All inputs are finite; a program needn't handle non-finite values.
Results may differ from the reference program's by a relative error of at most 0.0047.
Values may be sent and summed in bfloat16 or wider, within the bound.
No kernel may reach another device: no remote copies, remote signals or barrier semaphores. Data moves between devices by JAX's collectives and lax.ppermute only.
A program may use at most 64 MiB of HBM per device.

```python
import math
import jax
import jax.numpy as jnp
from jax import lax

D = 64
RHS = 16
ITERS = 2
TRAIN = 32768
CAND = 32768


def draw_targets(key, part):
    first, second = jax.random.split(key, 2)
    position = jnp.arange(TRAIN, dtype=jnp.float32) / max(TRAIN - 1, 1)
    column_scale = jnp.exp(jax.random.uniform(second, (TRAIN,), jnp.float32, 0.0, math.log(10.0))) * (0.5 + position) * 0.25
    base = jnp.clip(jax.random.normal(first, (RHS, TRAIN), jnp.float32), -4.0, 4.0)
    return base * column_scale[None, :]


def steps_of(own_key, dims, shards, least, high):
    def one(axis_at, blocks):
        draws = jax.random.uniform(jax.random.fold_in(jax.random.fold_in(own_key, 6), axis_at), (blocks,), jnp.float32, least / len(shards), high / len(shards))
        return jnp.repeat(jnp.exp(draws), dims[axis_at] // blocks).reshape((-1,) + (1,) * (len(dims) - axis_at - 1))

    loudness = one(*shards[0])
    for cut in shards[1:]:
        loudness = loudness * one(*cut)
    return loudness


def gaussian(own_key, extent, deviation, reach, pieces=(), held_as=jnp.bfloat16):
    gain = steps_of(own_key, extent, pieces, -0.22, 0.18) if pieces else 1.0
    entries = jax.random.normal(own_key, extent, jnp.float32) * deviation * gain
    return jnp.minimum(jnp.maximum(entries, -reach), reach).astype(held_as)


def setup_inputs(seed: int = 0) -> dict:
    key_list = jax.random.split(jax.random.key(seed), 6)
    train_points = gaussian(key_list[0], (D, TRAIN), 1.0, 6.0, ((1, 512),), jnp.float32)
    cand_points = gaussian(key_list[1], (D, CAND), 1.0, 6.0, ((1, 512),), jnp.float32)
    inv_length = jnp.clip(jnp.exp(jax.random.uniform(key_list[2], (D,), jnp.float32, math.log(0.04), math.log(0.7))), 0.04, 0.7)
    noise = jnp.clip(jnp.exp(math.log(4.0) - 2.0794415 * jax.random.uniform(key_list[3], (TRAIN,), jnp.float32) ** steps_of(key_list[3], (TRAIN,), ((0, 512),), -0.2, 0.2)), 0.5, 4.0)
    targets = draw_targets(jax.random.fold_in(key_list[5], 71), 0)
    return {"train_points": train_points, "cand_points": cand_points, "inv_length": inv_length, "noise": noise, "targets": targets}


root_five = math.sqrt(5.0)

def matern(left, left_norm, right, right_norm):
    inner = lax.dot_general(left, right, (((0,), (0,)), ((), ())), preferred_element_type=jnp.float32)
    dist_sq = jnp.maximum(left_norm[:, None] + right_norm[None, :] - 2.0 * inner, 0.0)
    radius = jnp.sqrt(dist_sq)
    return (1.0 + root_five * radius + 5.0 / 3.0 * dist_sq) * jnp.exp(-root_five * radius)

def kernel_apply(vector, points, norms, other, other_norms):
    size = points.shape[1]
    block = math.gcd(size, 512)

    def advance(total, index):
        offset = (index * block).astype(jnp.int32)
        sub_points = lax.dynamic_slice_in_dim(points, offset, block, 1)
        sub_norms = lax.dynamic_slice_in_dim(norms, offset, block, 0)
        sub_vector = lax.dynamic_slice_in_dim(vector, offset, block, 1)
        kernel_tile = matern(sub_points, sub_norms, other, other_norms)
        return (total + jnp.dot(sub_vector, kernel_tile, precision=lax.Precision.HIGHEST, preferred_element_type=jnp.float32), None)
    start_total = jnp.zeros((vector.shape[0], other.shape[1]), jnp.float32)
    total, _ = lax.scan(advance, start_total, jnp.arange(size // block, dtype=jnp.int32))
    return total

def reference(train_points, cand_points, inv_length, noise, targets):
    scaled_train = (train_points * inv_length[:, None]).astype(jnp.bfloat16)
    scaled_cand = (cand_points * inv_length[:, None]).astype(jnp.bfloat16)
    train_norms = lax.optimization_barrier(jnp.sum(jnp.square(scaled_train.astype(jnp.float32)), axis=0))
    cand_norms = lax.optimization_barrier(jnp.sum(jnp.square(scaled_cand.astype(jnp.float32)), axis=0))
    solution = jnp.zeros_like(targets)
    residual = targets
    direction = targets
    norm_now = lax.optimization_barrier(jnp.sum(residual * residual, axis=1))
    for iteration in range(ITERS):
        image = kernel_apply(direction, scaled_train, train_norms, scaled_train, train_norms) + noise[None, :] * direction
        alpha = norm_now / lax.optimization_barrier(jnp.sum(direction * image, axis=1))
        solution = solution + alpha[:, None] * direction
        residual = residual - alpha[:, None] * image
        norm_next = lax.optimization_barrier(jnp.sum(residual * residual, axis=1))
        direction = residual + (norm_next / norm_now)[:, None] * direction
        norm_now = norm_next
    post_mean = kernel_apply(solution, scaled_train, train_norms, scaled_cand, cand_norms)
    return (solution, post_mean)
```

```python
import functools
import math

import jax
import jax.numpy as jnp
from jax import lax
from jax.experimental import pallas as pl
from jax.experimental.pallas import tpu as pltpu
from jax.sharding import Mesh, PartitionSpec as P

F32 = jnp.float32
BF16 = jnp.bfloat16

D = 64
S = 64
RHS = 16
NQ = 16
NZ = 16
ROWS = NQ * S
COLS = 2 * NZ * S
LOG2E = math.log2(math.e)
PARAMS = pltpu.CompilerParams(vmem_limit_bytes=24 * 1024 * 1024)


def halves(value):
    high = value.astype(BF16)
    return high, (value - high.astype(F32)).astype(BF16)


def thirds(value):
    high = value.astype(BF16).astype(F32)
    rest = value - high
    middle = rest.astype(BF16).astype(F32)
    low = (rest - middle).astype(BF16).astype(F32)
    return high, middle, low


def rows_of(width, pieces):
    index = lax.broadcasted_iota(jnp.int32, (16, width), 0)
    total = jnp.zeros((16, width), F32)
    for i, piece in enumerate(pieces):
        total = jnp.where(index == i, piece, total)
    return total


def column(row, start):
    lane = lax.broadcasted_iota(jnp.int32, (RHS, 128), 1)
    index = lax.broadcasted_iota(jnp.int32, (RHS, 128), 0)
    return jnp.sum(jnp.where(lane == index + start, row, 0.0), axis=1, keepdims=True)


def prepare(train_ref, cand_ref, inv_ref, target_ref, y_ref, z_ref):
    eye = lax.broadcasted_iota(jnp.int32, (D, D), 0) == lax.broadcasted_iota(
        jnp.int32, (D, D), 1
    )
    inv = jnp.sum(jnp.where(eye, inv_ref[...], 0.0), axis=1, keepdims=True)
    train = train_ref[...] * inv
    cand = cand_ref[...] * inv
    b_high, b_low = halves(target_ref[...])
    b = jnp.concatenate([b_high, b_low], axis=1)
    both = jnp.concatenate([train.astype(BF16), cand.astype(BF16)], axis=1)
    folded = jnp.concatenate([train[:32].astype(BF16), train[32:].astype(BF16)], axis=1)
    for i in range(NQ):
        y_ref[i, 0:64, :] = both
        y_ref[i, 64:80, :] = b
        z_ref[i, 0:32, :] = folded
        z_ref[i, 32:48, :] = b


def row_side(y_ref, j, first):
    points = jnp.concatenate(
        [y_ref[2 * j, 0:64, first : first + 64], y_ref[2 * j + 1, 0:64, first : first + 64]],
        axis=1,
    ).astype(F32)
    norm = jnp.sum(points * points, axis=0, keepdims=True)
    extra = rows_of(128, [*thirds(norm), 1.0, 1.0, 1.0])
    return jnp.concatenate(
        [-2.0 * points, extra, jnp.zeros((48, 128), F32)], axis=0
    ).astype(BF16)


def col_side(z_ref, z):
    low = z_ref[0, z, 0:32, :]
    high = z_ref[1, z, 0:32, :]
    points = jnp.concatenate(
        [
            jnp.concatenate([low[:, :64], high[:, :64]], axis=1),
            jnp.concatenate([low[:, 64:], high[:, 64:]], axis=1),
        ],
        axis=0,
    ).astype(F32)
    norm = jnp.sum(points * points, axis=0, keepdims=True)
    extra = rows_of(128, [1.0, 1.0, 1.0, *thirds(norm)])
    full = jnp.concatenate([points, extra, jnp.zeros((48, 128), F32)], axis=0)
    return full.T.astype(BF16)


def matern_of(inner):
    five_dist = jnp.maximum(inner, 1e-30) * 5.0
    scaled = five_dist * lax.rsqrt(five_dist)
    return (1.0 + scaled + five_dist * (1.0 / 3.0)) * jnp.exp2(scaled * (-LOG2E))


def tile(points, b, row_aug, kern_ref, acc_ref, z):
    offset = pl.multiple_of(z * 128, 128)
    for part in range(ROWS // 256):
        span = slice(part * 256, part * 256 + 256)
        inner = jnp.dot(points, row_aug[:, span], preferred_element_type=F32)
        kern = matern_of(inner).astype(BF16)
        kern_ref[pl.ds(offset, 128), span] = kern
        acc_ref[:, span] += jnp.dot(b, kern, preferred_element_type=F32)


def own_block(q):
    return pl.ds(pl.multiple_of((q // 2) * 128, 128), 128)


def own_mask(q):
    lane = lax.broadcasted_iota(jnp.int32, (RHS, 128), 1)
    return (lane // 64) == (q % 2)


def position():
    return lax.axis_index("y") * 4 + lax.axis_index("x")


def first_apply(
    y_ref, z_ref, target_ref, noise_ref, kern_ref, col_ref, b_ref, out_ref, acc_ref, row_ref
):
    q = position()
    for j in range(NQ // 2):
        row_ref[:, j * 128 : j * 128 + 128] = row_side(y_ref, j, 0)
    acc_ref[...] = jnp.zeros_like(acc_ref)

    def step(z, _):
        points = col_side(z_ref, z)
        offset = pl.multiple_of(z * 128, 128)
        col_ref[pl.ds(offset, 128), :] = points
        low, high = z_ref[0, z, 32:48, :], z_ref[1, z, 32:48, :]
        b = jnp.concatenate(
            [
                jnp.concatenate([low[:, :64], high[:, :64]], axis=1),
                jnp.concatenate([low[:, 64:], high[:, 64:]], axis=1),
            ],
            axis=0,
        )
        b_ref[z] = b
        tile(points, b, row_ref, kern_ref, acc_ref, z)
        return 0

    lax.fori_loop(0, NZ, step, 0)
    own = target_ref[...] * noise_ref[...]
    twice = jnp.concatenate([own, own], axis=1)
    acc_ref[0:16, own_block(q)] += jnp.where(own_mask(q), twice, 0.0)
    image = (acc_ref[0:16, :] + acc_ref[16:32, :]).astype(BF16)
    for i in range(NQ):
        out_ref[i] = image


def cand_apply(y_ref, col_ref, b_ref, kern_ref, out_ref, acc_ref, row_ref):
    for j in range(NQ // 2):
        row_ref[:, j * 128 : j * 128 + 128] = row_side(y_ref, j, 64)
    acc_ref[...] = jnp.zeros_like(acc_ref)

    def step(z, _):
        offset = pl.multiple_of(z * 128, 128)
        tile(col_ref[pl.ds(offset, 128), :], b_ref[z], row_ref, kern_ref, acc_ref, z)
        return 0

    lax.fori_loop(0, NZ, step, 0)
    out_ref[...] = acc_ref[0:16, :] + acc_ref[16:32, :]


def merge_image(part_ref, y_ref, out_ref, w_ref, br_ref):
    q = position()
    total = part_ref[0].astype(F32)
    for i in range(1, NQ):
        total = total + part_ref[i].astype(F32)
    w_ref[...] = total
    for j in range(NQ // 2):
        even, odd = y_ref[2 * j, 64:80, :].astype(F32), y_ref[2 * j + 1, 64:80, :].astype(F32)
        br_ref[:, j * 128 : j * 128 + 128] = jnp.concatenate(
            [even[:, :64] + even[:, 64:], odd[:, :64] + odd[:, 64:]], axis=1
        )
    b = br_ref[...]
    bw = jnp.sum(b * total, axis=1, keepdims=True)
    bb = jnp.sum(b * b, axis=1, keepdims=True)
    block = w_ref[:, own_block(q)]
    own = jnp.where(q % 2 == 0, block[:, :64], block[:, 64:])
    lane = lax.broadcasted_iota(jnp.int32, (RHS, 64), 1)
    scalars = jnp.zeros((RHS, 64), F32)
    for i, piece in enumerate([*thirds(bw), *thirds(bb)]):
        scalars = jnp.where(lane == i, piece, scalars)
    message = jnp.concatenate([own, scalars], axis=1).astype(BF16)
    for i in range(NZ):
        out_ref[i] = message


def second_apply(
    s_ref, b_ref, w_ref, br_ref, kern_ref, cand_ref, mean_ref, target_ref, noise_ref,
    out_ref, own_ref, r_ref,
):
    q = position()
    sums = s_ref[0, 0, :, 64:128].astype(F32)
    for c in range(2):
        for z in range(NZ):
            if c or z:
                sums = sums + s_ref[c, z, :, 64:128].astype(F32)
    lane = lax.broadcasted_iota(jnp.int32, (RHS, 64), 1)
    bw = jnp.sum(jnp.where(lane < 3, sums, 0.0), axis=1, keepdims=True)
    bb = jnp.sum(jnp.where((lane >= 3) & (lane < 6), sums, 0.0), axis=1, keepdims=True)
    alpha = bb / bw
    for z in range(NZ):
        w = jnp.concatenate([s_ref[0, z, :, 0:64], s_ref[1, z, :, 0:64]], axis=1).astype(F32)
        b = b_ref[z, 0:16, :].astype(F32) + b_ref[z, 16:32, :].astype(F32)
        high, low = halves(b - alpha * w)
        r_ref[:, z * 128 : z * 128 + 128] = jnp.concatenate([high, low], axis=0)
    r = r_ref[...]
    applied = jnp.dot(r, kern_ref[...], preferred_element_type=F32)
    applied = applied[0:16] + applied[16:32]
    mean = jnp.dot(r, cand_ref[...], preferred_element_type=F32)
    mean = mean[0:16] + mean[16:32]
    mean0 = mean_ref[...]
    for i in range(NQ):
        span = slice(i * 64, i * 64 + 64)
        out_ref[i, 0:16, :] = jnp.concatenate([mean0[:, span], mean[:, span]], axis=1)
    r_row = br_ref[...] - alpha * w_ref[...]
    block = w_ref[:, own_block(q)]
    own_w = jnp.where(q % 2 == 0, block[:, :64], block[:, 64:])
    target = target_ref[...]
    own_r = target - alpha * own_w
    s = jnp.sum(r_row * applied, axis=1, keepdims=True) + jnp.sum(
        noise_ref[...] * own_r * own_r, axis=1, keepdims=True
    )
    t = jnp.sum(own_r * own_w, axis=1, keepdims=True)
    rr = jnp.sum(own_r * own_r, axis=1, keepdims=True)
    wide = lax.broadcasted_iota(jnp.int32, (RHS, 128), 1)
    index = lax.broadcasted_iota(jnp.int32, (RHS, 128), 0)
    spread = (
        jnp.where(wide == index, s, 0.0)
        + jnp.where(wide == index + 16, t, 0.0)
        + jnp.where(wide == index + 32, rr, 0.0)
    )
    spread = jnp.sum(spread, axis=0, keepdims=True)
    eight = lax.broadcasted_iota(jnp.int32, (8, 128), 0)
    spread = jnp.where(eight == 0, spread, 0.0)
    for i in range(NQ):
        out_ref[i, 16:24, :] = spread
    side = jnp.where(lane == 0, bb, jnp.where(lane == 1, bw, 0.0))
    own_ref[...] = jnp.concatenate([own_r, side], axis=1)


def merge_mean(part_ref, mean_ref, out_ref):
    total = part_ref[0]
    for i in range(1, NQ):
        total = total + part_ref[i]
    mean_ref[...] = total[0:16]
    for i in range(NZ):
        out_ref[i] = total[16:17]


def finish(s_ref, own_ref, mean_ref, target_ref, solution_ref, post_ref):
    total = s_ref[0, 0]
    for c in range(2):
        for z in range(NZ):
            if c or z:
                total = total + s_ref[c, z]
    s, t, rr = column(total, 0), column(total, 16), column(total, 32)
    own_r = own_ref[:, 0:64]
    bb, bw = own_ref[:, 64:65], own_ref[:, 65:66]
    alpha0 = bb / bw
    beta = rr / bb
    alpha1 = rr / (s + 2.0 * beta * t + beta * beta * bw)
    target = target_ref[...]
    solution_ref[...] = alpha0 * target + alpha1 * (own_r + beta * target)
    mean = mean_ref[...]
    post_ref[...] = (alpha0 + alpha1 * beta) * mean[:, :64] + alpha1 * mean[:, 64:]


def shape(*dims, dtype=F32):
    return jax.ShapeDtypeStruct(dims, dtype)


def per_device(train_points, cand_points, inv_length, noise, targets):
    noise = noise.reshape(1, S)
    call = functools.partial(pl.pallas_call, compiler_params=PARAMS)
    y_out, z_out = call(
        prepare,
        out_shape=(shape(NQ, 80, 128, dtype=BF16), shape(NZ, 48, 128, dtype=BF16)),
    )(train_points, cand_points, inv_length.reshape(1, D), targets)
    y_in = lax.all_to_all(y_out, ("y", "x"), 0, 0)
    z_in = lax.all_gather(lax.all_to_all(z_out, "z", 0, 0), "c", axis=0)
    cost = pl.CostEstimate(
        flops=2 * ROWS * COLS * 160, bytes_accessed=2 * ROWS * COLS, transcendentals=2 * ROWS * COLS
    )
    kern, col, b_col, image_out = call(
        first_apply,
        out_shape=(
            shape(COLS, ROWS, dtype=BF16),
            shape(COLS, 128, dtype=BF16),
            shape(NZ, 32, 128, dtype=BF16),
            shape(NQ, RHS, ROWS, dtype=BF16),
        ),
        scratch_shapes=[pltpu.VMEM((32, ROWS), F32), pltpu.VMEM((128, ROWS), BF16)],
        cost_estimate=cost,
    )(y_in, z_in, targets, noise)
    image_in = lax.all_to_all(image_out, ("y", "x"), 0, 0)
    kern_cand, mean0 = call(
        cand_apply,
        out_shape=(shape(COLS, ROWS, dtype=BF16), shape(RHS, ROWS)),
        scratch_shapes=[pltpu.VMEM((32, ROWS), F32), pltpu.VMEM((128, ROWS), BF16)],
        cost_estimate=cost,
    )(y_in, col, b_col)
    w_out, w_row, b_row = call(
        merge_image,
        out_shape=(shape(NZ, RHS, 128, dtype=BF16), shape(RHS, ROWS), shape(RHS, ROWS)),
    )(image_in, y_in)
    w_in = lax.all_gather(lax.all_to_all(w_out, "z", 0, 0), "c", axis=0)
    mean_out, own = call(
        second_apply,
        out_shape=(shape(NQ, 24, 128), shape(RHS, 128)),
        scratch_shapes=[pltpu.VMEM((32, COLS), BF16)],
    )(w_in, b_col, w_row, b_row, kern, kern_cand, mean0, targets, noise)
    mean_in = lax.all_to_all(mean_out, ("y", "x"), 0, 0)
    mean, scalar_out = call(
        merge_mean, out_shape=(shape(RHS, 128), shape(NZ, 1, 128))
    )(mean_in)
    scalar_in = lax.all_gather(lax.all_to_all(scalar_out, "z", 0, 0), "c", axis=0)
    return call(finish, out_shape=(shape(RHS, S), shape(RHS, S)))(
        scalar_in, own, mean, targets
    )


def solution(mesh):
    fine = Mesh(mesh.devices.reshape(16, 2, 4, 4), ("z", "c", "y", "x"))
    every = ("z", "c", "y", "x")
    wide = P(None, every)
    return jax.shard_map(
        per_device,
        mesh=fine,
        in_specs=(wide, wide, P(), P(every), wide),
        out_specs=(wide, wide),
        check_vma=False,
    )
```

```python
import math

import jax
import jax.numpy as jnp
from jax import lax
from jax.experimental import pallas as pl
from jax.experimental.pallas import tpu as pltpu
from jax.sharding import Mesh, PartitionSpec as P

F32 = jnp.float32
BF16 = jnp.bfloat16

D = 64
S = 64
RHS = 16
NQ = 16
NZ = 16
ROWS = NQ * S
COLS = 2 * NZ * S
LOG2E = math.log2(math.e)
CHUNKS = 8
PIECE = COLS // CHUNKS
SMALL = pltpu.CompilerParams(vmem_limit_bytes=24 * 1024 * 1024)
LARGE = pltpu.CompilerParams(vmem_limit_bytes=63_000_000)


def halves(value):
    high = value.astype(BF16)
    return high, (value - high.astype(F32)).astype(BF16)


def thirds(value):
    high = value.astype(BF16).astype(F32)
    rest = value - high
    middle = rest.astype(BF16).astype(F32)
    low = (rest - middle).astype(BF16).astype(F32)
    return high, middle, low


def rows_of(width, pieces):
    index = lax.broadcasted_iota(jnp.int32, (16, width), 0)
    total = jnp.zeros((16, width), F32)
    for i, piece in enumerate(pieces):
        total = jnp.where(index == i, piece, total)
    return total


def column(row, start):
    lane = lax.broadcasted_iota(jnp.int32, (RHS, 128), 1)
    index = lax.broadcasted_iota(jnp.int32, (RHS, 128), 0)
    return jnp.sum(jnp.where(lane == index + start, row, 0.0), axis=1, keepdims=True)


def prepare(
    train_hbm, cand_hbm, inv_hbm, noise_hbm, target_hbm, y_ref, z_ref, side_ref,
    train_ref, cand_ref, inv_ref, noise_ref, target_ref, sems,
):
    copies = [
        pltpu.make_async_copy(source, target, sems.at[i])
        for i, (source, target) in enumerate(
            [
                (train_hbm, train_ref),
                (inv_hbm, inv_ref),
                (target_hbm, target_ref),
                (cand_hbm, cand_ref),
                (noise_hbm, noise_ref),
            ]
        )
    ]
    for copy in copies:
        copy.start()
    for copy in copies:
        copy.wait()
    eye = lax.broadcasted_iota(jnp.int32, (D, D), 0) == lax.broadcasted_iota(
        jnp.int32, (D, D), 1
    )
    inv = jnp.sum(jnp.where(eye, inv_ref[...], 0.0), axis=1, keepdims=True)
    train = train_ref[...] * inv
    cand = cand_ref[...] * inv
    target = target_ref[...]
    b_high, b_low = halves(target)
    b = jnp.concatenate([b_high, b_low], axis=1)
    both = jnp.concatenate([train.astype(BF16), cand.astype(BF16)], axis=1)
    folded = jnp.concatenate([train[:32].astype(BF16), train[32:].astype(BF16)], axis=1)
    for i in range(NQ):
        z_ref[i, 0:32, :] = folded
        z_ref[i, 32:48, :] = b
        y_ref[i, 0:64, :] = both
        y_ref[i, 64:80, :] = b
    side_ref[...] = jnp.concatenate(
        [target, jnp.broadcast_to(noise_ref[...], (RHS, S))], axis=1
    )


def row_side(y_ref, j, first):
    points = jnp.concatenate(
        [y_ref[2 * j, 0:64, first : first + 64], y_ref[2 * j + 1, 0:64, first : first + 64]],
        axis=1,
    ).astype(F32)
    norm = jnp.sum(points * points, axis=0, keepdims=True)
    extra = rows_of(128, [*thirds(norm), 1.0, 1.0, 1.0])
    return jnp.concatenate(
        [-2.0 * points, extra, jnp.zeros((48, 128), F32)], axis=0
    ).astype(BF16)


def col_side(z_ref, col_ref, b_ref):
    for z in range(NZ):
        low, high = z_ref[0, z, 0:48, :], z_ref[1, z, 0:48, :]
        first = jnp.concatenate([low[:, :64], high[:, :64]], axis=1)
        second = jnp.concatenate([low[:, 64:], high[:, 64:]], axis=1)
        points = jnp.concatenate([first[0:32], second[0:32]], axis=0).astype(F32)
        b_ref[:, z * 128 : z * 128 + 128] = jnp.concatenate([first[32:48], second[32:48]], axis=0)
        norm = jnp.sum(points * points, axis=0, keepdims=True)
        extra = rows_of(128, [1.0, 1.0, 1.0, *thirds(norm)])
        full = jnp.concatenate([points, extra, jnp.zeros((48, 128), F32)], axis=0)
        col_ref[z * 128 : z * 128 + 128, :] = full.T.astype(BF16)


def matern_of(inner):
    five_dist = jnp.maximum(inner, 1e-30) * 5.0
    scaled = five_dist * lax.rsqrt(five_dist)
    return (1.0 + scaled + five_dist * (1.0 / 3.0)) * jnp.exp2(scaled * (-LOG2E))


def piece(tile_ref, hbm_ref, sems, i):
    span = pl.ds(pl.multiple_of(i * PIECE, PIECE), PIECE)
    return tile_ref.at[span, :], hbm_ref.at[span, :], sems.at[i]


def fill(col_ref, row_ref, kern_ref, hbm_ref, sems, even_ref, odd_ref):
    def inner(z, out_ref):
        points = col_ref[pl.ds(pl.multiple_of(z * 128, 128), 128), :]
        out_ref[...] = jnp.dot(points, row_ref[...], preferred_element_type=F32)

    def spread(z, in_ref):
        for i in range(8):
            kern_ref[pl.ds(pl.multiple_of(z * 128 + i * 16, 16), 16), :] = matern_of(
                in_ref[i * 16 : i * 16 + 16, :]
            ).astype(BF16)

    inner(0, even_ref)

    def send(i):
        pltpu.make_async_copy(*piece(kern_ref, hbm_ref, sems, i)).start()

    def step(i, _):
        @pl.when(i > 0)
        def _():
            send(i - 1)

        inner(2 * i + 1, odd_ref)
        spread(2 * i, even_ref)
        inner(jnp.minimum(2 * i + 2, NZ - 1), even_ref)
        spread(2 * i + 1, odd_ref)
        return 0

    lax.fori_loop(0, NZ // 2, step, 0)


def finish_fill(kern_ref, hbm_ref, sems):
    for i in range(CHUNKS):
        pltpu.make_async_copy(*piece(kern_ref, hbm_ref, sems, i)).wait()


def apply(vectors, kern_ref):
    total = jnp.dot(vectors, kern_ref[...], preferred_element_type=F32)
    return total[0:16] + total[16:32]


def own_block(q):
    return pl.ds(pl.multiple_of((q // 2) * 128, 128), 128)


def own_mask(q):
    lane = lax.broadcasted_iota(jnp.int32, (RHS, 128), 1)
    return (lane // 64) == (q % 2)


def position():
    return lax.axis_index("y") * 4 + lax.axis_index("x")


def first_apply(
    y_ref, col_ref, b_ref, side_ref, hbm_ref, out_ref,
    acc_ref, row_ref, even_ref, odd_ref, kern_ref, sems,
):
    q = position()
    for j in range(NQ // 2):
        row_ref[:, j * 128 : j * 128 + 128] = row_side(y_ref, j, 0)
    fill(col_ref, row_ref, kern_ref, hbm_ref, sems, even_ref, odd_ref)
    acc_ref[...] = apply(b_ref[...], kern_ref)
    pltpu.make_async_copy(*piece(kern_ref, hbm_ref, sems, CHUNKS - 1)).start()
    own = side_ref[:, 0:64] * side_ref[:, 64:128]
    twice = jnp.concatenate([own, own], axis=1)
    acc_ref[:, own_block(q)] += jnp.where(own_mask(q), twice, 0.0)
    image = acc_ref[...].astype(BF16)
    for i in range(NQ):
        out_ref[i] = image
    finish_fill(kern_ref, hbm_ref, sems)


def cand_apply(
    y_ref, col_ref, b_ref, hbm_ref, out_ref, row_ref, even_ref, odd_ref, kern_ref, sems
):
    for j in range(NQ // 2):
        row_ref[:, j * 128 : j * 128 + 128] = row_side(y_ref, j, 64)
    fill(col_ref, row_ref, kern_ref, hbm_ref, sems, even_ref, odd_ref)
    out_ref[...] = apply(b_ref[...], kern_ref)
    pltpu.make_async_copy(*piece(kern_ref, hbm_ref, sems, CHUNKS - 1)).start()
    finish_fill(kern_ref, hbm_ref, sems)


def merge_image(part_ref, y_ref, out_ref, w_ref, br_ref):
    q = position()
    total = part_ref[0].astype(F32)
    for i in range(1, NQ):
        total = total + part_ref[i].astype(F32)
    w_ref[...] = total
    for j in range(NQ // 2):
        even, odd = y_ref[2 * j, 64:80, :].astype(F32), y_ref[2 * j + 1, 64:80, :].astype(F32)
        br_ref[:, j * 128 : j * 128 + 128] = jnp.concatenate(
            [even[:, :64] + even[:, 64:], odd[:, :64] + odd[:, 64:]], axis=1
        )
    b = br_ref[...]
    bw = jnp.sum(b * total, axis=1, keepdims=True)
    bb = jnp.sum(b * b, axis=1, keepdims=True)
    block = w_ref[:, own_block(q)]
    own = jnp.where(q % 2 == 0, block[:, :64], block[:, 64:])
    lane = lax.broadcasted_iota(jnp.int32, (RHS, 64), 1)
    scalars = jnp.zeros((RHS, 64), F32)
    for i, piece in enumerate([*thirds(bw), *thirds(bb)]):
        scalars = jnp.where(lane == i, piece, scalars)
    message = jnp.concatenate([own, scalars], axis=1).astype(BF16)
    for i in range(NZ):
        out_ref[i] = message


def second_apply(
    s_ref, b_ref, w_ref, br_ref, kern_hbm, cand_hbm, mean_ref, side_ref, out_ref, own_ref,
    r_ref, kern_ref, cand_ref, kern_sems, cand_sems,
):
    def fetch(hbm_ref, tile_ref, sems, i):
        target, source, sem = piece(tile_ref, hbm_ref, sems, i)
        return pltpu.make_async_copy(source, target, sem)

    for i in range(CHUNKS):
        fetch(kern_hbm, kern_ref, kern_sems, i).start()
    for i in range(CHUNKS):
        fetch(cand_hbm, cand_ref, cand_sems, i).start()
    q = position()
    sums = s_ref[0, 0, :, 64:128].astype(F32)
    for c in range(2):
        for z in range(NZ):
            if c or z:
                sums = sums + s_ref[c, z, :, 64:128].astype(F32)
    lane = lax.broadcasted_iota(jnp.int32, (RHS, 64), 1)
    bw = jnp.sum(jnp.where(lane < 3, sums, 0.0), axis=1, keepdims=True)
    bb = jnp.sum(jnp.where((lane >= 3) & (lane < 6), sums, 0.0), axis=1, keepdims=True)
    alpha = bb / bw
    for z in range(NZ):
        w = jnp.concatenate([s_ref[0, z, :, 0:64], s_ref[1, z, :, 0:64]], axis=1).astype(F32)
        span = slice(z * 128, z * 128 + 128)
        b = b_ref[0:16, span].astype(F32) + b_ref[16:32, span].astype(F32)
        high, low = halves(b - alpha * w)
        r_ref[:, span] = jnp.concatenate([high, low], axis=0)
    def gathered(hbm_ref, tile_ref, sems):
        total = None
        for i in range(CHUNKS):
            fetch(hbm_ref, tile_ref, sems, i).wait()
            span = slice(i * PIECE, i * PIECE + PIECE)
            part = jnp.dot(r_ref[:, span], tile_ref[span, :], preferred_element_type=F32)
            total = part if total is None else total + part
        return total[0:16] + total[16:32]

    applied = gathered(kern_hbm, kern_ref, kern_sems)
    mean = gathered(cand_hbm, cand_ref, cand_sems)
    mean0 = mean_ref[...]
    for i in range(NQ):
        span = slice(i * 64, i * 64 + 64)
        out_ref[i, 0:16, :] = jnp.concatenate([mean0[:, span], mean[:, span]], axis=1)
    r_row = br_ref[...] - alpha * w_ref[...]
    block = w_ref[:, own_block(q)]
    own_w = jnp.where(q % 2 == 0, block[:, :64], block[:, 64:])
    target, noise = side_ref[:, 0:64], side_ref[:, 64:128]
    own_r = target - alpha * own_w
    s = jnp.sum(r_row * applied, axis=1, keepdims=True) + jnp.sum(
        noise * own_r * own_r, axis=1, keepdims=True
    )
    t = jnp.sum(own_r * own_w, axis=1, keepdims=True)
    rr = jnp.sum(own_r * own_r, axis=1, keepdims=True)
    wide = lax.broadcasted_iota(jnp.int32, (RHS, 128), 1)
    index = lax.broadcasted_iota(jnp.int32, (RHS, 128), 0)
    spread = (
        jnp.where(wide == index, s, 0.0)
        + jnp.where(wide == index + 16, t, 0.0)
        + jnp.where(wide == index + 32, rr, 0.0)
    )
    spread = jnp.sum(spread, axis=0, keepdims=True)
    eight = lax.broadcasted_iota(jnp.int32, (8, 128), 0)
    spread = jnp.where(eight == 0, spread, 0.0)
    for i in range(NQ):
        out_ref[i, 16:24, :] = spread
    side = jnp.where(lane == 0, bb, jnp.where(lane == 1, bw, 0.0))
    own_ref[...] = jnp.concatenate([own_r, side], axis=1)


def merge_mean(part_ref, mean_ref, out_ref):
    total = part_ref[0]
    for i in range(1, NQ):
        total = total + part_ref[i]
    mean_ref[...] = total[0:16]
    for i in range(NZ):
        out_ref[i] = total[16:17]


def finish(s_ref, own_ref, mean_ref, side_ref, solution_ref, post_ref):
    total = s_ref[0, 0]
    for c in range(2):
        for z in range(NZ):
            if c or z:
                total = total + s_ref[c, z]
    s, t, rr = column(total, 0), column(total, 16), column(total, 32)
    own_r = own_ref[:, 0:64]
    bb, bw = own_ref[:, 64:65], own_ref[:, 65:66]
    alpha0 = bb / bw
    beta = rr / bb
    alpha1 = rr / (s + 2.0 * beta * t + beta * beta * bw)
    target = side_ref[:, 0:64]
    solution_ref[...] = alpha0 * target + alpha1 * (own_r + beta * target)
    mean = mean_ref[...]
    post_ref[...] = (alpha0 + alpha1 * beta) * mean[:, :64] + alpha1 * mean[:, 64:]


def shape(*dims, dtype=F32):
    return jax.ShapeDtypeStruct(dims, dtype)


def per_device(train_points, cand_points, inv_length, noise, targets):
    call = pl.pallas_call
    y_out, z_out, side = call(
        prepare,
        in_specs=[pl.BlockSpec(memory_space=pltpu.HBM)] * 5,
        out_shape=(
            shape(NQ, 80, 128, dtype=BF16),
            shape(NZ, 48, 128, dtype=BF16),
            shape(RHS, 128),
        ),
        scratch_shapes=[
            pltpu.VMEM((D, S), F32),
            pltpu.VMEM((D, S), F32),
            pltpu.VMEM((1, D), F32),
            pltpu.VMEM((1, S), F32),
            pltpu.VMEM((RHS, S), F32),
            pltpu.SemaphoreType.DMA((5,)),
        ],
        compiler_params=pltpu.CompilerParams(vmem_limit_bytes=67043328),
    )(train_points, cand_points, inv_length.reshape(1, D), noise.reshape(1, S), targets)
    z_in = lax.all_gather(lax.all_to_all(z_out, "z", 0, 0), "c", axis=0)
    y_in = lax.all_to_all(y_out, ("y", "x"), 0, 0)
    col, b_col = call(
        col_side,
        compiler_params=SMALL,
        out_shape=(shape(COLS, 128, dtype=BF16), shape(32, COLS, dtype=BF16)),
        cost_estimate=pl.CostEstimate(
            flops=COLS * 1000, bytes_accessed=4 * COLS * 128, transcendentals=0
        ),
    )(z_in)
    cost = pl.CostEstimate(
        flops=2 * ROWS * COLS * 160, bytes_accessed=2 * ROWS * COLS, transcendentals=2 * ROWS * COLS
    )
    tiles = [
        pltpu.VMEM((128, ROWS), BF16),
        pltpu.VMEM((128, ROWS), F32),
        pltpu.VMEM((128, ROWS), F32),
        pltpu.VMEM((COLS, ROWS), BF16),
        pltpu.SemaphoreType.DMA((CHUNKS,)),
    ]
    vmem = pl.BlockSpec(memory_space=pltpu.VMEM)
    anywhere = pl.BlockSpec(memory_space=pl.ANY)
    kern, image_out = call(
        first_apply,
        compiler_params=LARGE,
        in_specs=[vmem] * 4,
        out_specs=(anywhere, vmem),
        out_shape=(
            shape(COLS, ROWS, dtype=BF16),
            shape(NQ, RHS, ROWS, dtype=BF16),
        ),
        scratch_shapes=[pltpu.VMEM((RHS, ROWS), F32), *tiles],
        cost_estimate=cost,
    )(y_in, col, b_col, side)
    image_in = lax.all_to_all(image_out, ("y", "x"), 0, 0)
    kern_cand, mean0 = call(
        cand_apply,
        compiler_params=LARGE,
        in_specs=[vmem] * 3,
        out_specs=(anywhere, vmem),
        out_shape=(shape(COLS, ROWS, dtype=BF16), shape(RHS, ROWS)),
        scratch_shapes=tiles,
        cost_estimate=cost,
    )(y_in, col, b_col)
    w_out, w_row, b_row = call(
        merge_image,
        compiler_params=SMALL,
        out_shape=(shape(NZ, RHS, 128, dtype=BF16), shape(RHS, ROWS), shape(RHS, ROWS)),
    )(image_in, y_in)
    w_in = lax.all_gather(lax.all_to_all(w_out, "z", 0, 0), "c", axis=0)
    mean_out, own = call(
        second_apply,
        compiler_params=LARGE,
        in_specs=[vmem] * 4 + [anywhere] * 2 + [vmem] * 2,
        out_shape=(shape(NQ, 24, 128), shape(RHS, 128)),
        scratch_shapes=[
            pltpu.VMEM((32, COLS), BF16),
            pltpu.VMEM((COLS, ROWS), BF16),
            pltpu.VMEM((COLS, ROWS), BF16),
            pltpu.SemaphoreType.DMA((CHUNKS,)),
            pltpu.SemaphoreType.DMA((CHUNKS,)),
        ],
    )(w_in, b_col, w_row, b_row, kern, kern_cand, mean0, side)
    mean_in = lax.all_to_all(mean_out, ("y", "x"), 0, 0)
    mean, scalar_out = call(
        merge_mean,
        compiler_params=SMALL,
        out_shape=(shape(RHS, 128), shape(NZ, 1, 128)),
    )(mean_in)
    scalar_in = lax.all_gather(lax.all_to_all(scalar_out, "z", 0, 0), "c", axis=0)
    return call(
        finish, compiler_params=SMALL, out_shape=(shape(RHS, S), shape(RHS, S))
    )(
        scalar_in, own, mean, side
    )


def solution(mesh):
    fine = Mesh(mesh.devices.reshape(16, 2, 4, 4), ("z", "c", "y", "x"))
    every = ("z", "c", "y", "x")
    wide = P(None, every)
    return jax.shard_map(
        per_device,
        mesh=fine,
        in_specs=(wide, wide, P(), P(every), wide),
        out_specs=(wide, wide),
        check_vma=False,
    )
```

```python
import math

import jax
import jax.numpy as jnp
from jax import lax
from jax.experimental import pallas as pl
from jax.experimental.pallas import tpu as pltpu
from jax.sharding import Mesh, PartitionSpec as P

F32 = jnp.float32
BF16 = jnp.bfloat16

D = 64
S = 64
RHS = 16
NQ = 16
NZ = 16
ROWS = NQ * S
COLS = 2 * NZ * S
LOG2E = math.log2(math.e)
CHUNKS = 8
PIECE = COLS // CHUNKS
PARAMS = pltpu.CompilerParams(vmem_limit_bytes=24 * 1024 * 1024)


def halves(value):
    high = value.astype(BF16)
    return high, (value - high.astype(F32)).astype(BF16)


def thirds(value):
    high = value.astype(BF16).astype(F32)
    rest = value - high
    middle = rest.astype(BF16).astype(F32)
    low = (rest - middle).astype(BF16).astype(F32)
    return high, middle, low


def rows_of(width, pieces):
    index = lax.broadcasted_iota(jnp.int32, (16, width), 0)
    total = jnp.zeros((16, width), F32)
    for i, piece in enumerate(pieces):
        total = jnp.where(index == i, piece, total)
    return total


def column(row, start):
    lane = lax.broadcasted_iota(jnp.int32, (RHS, 128), 1)
    index = lax.broadcasted_iota(jnp.int32, (RHS, 128), 0)
    return jnp.sum(jnp.where(lane == index + start, row, 0.0), axis=1, keepdims=True)


def prepare(
    train_hbm, cand_hbm, inv_hbm, noise_hbm, target_hbm, y_ref, z_ref, side_ref,
    train_ref, cand_ref, inv_ref, noise_ref, target_ref, sems,
):
    copies = [
        pltpu.make_async_copy(source, target, sems.at[i])
        for i, (source, target) in enumerate(
            [
                (train_hbm, train_ref),
                (inv_hbm, inv_ref),
                (target_hbm, target_ref),
                (cand_hbm, cand_ref),
                (noise_hbm, noise_ref),
            ]
        )
    ]
    for copy in copies:
        copy.start()
    for copy in copies:
        copy.wait()
    eye = lax.broadcasted_iota(jnp.int32, (D, D), 0) == lax.broadcasted_iota(
        jnp.int32, (D, D), 1
    )
    inv = jnp.sum(jnp.where(eye, inv_ref[...], 0.0), axis=1, keepdims=True)
    train = train_ref[...] * inv
    cand = cand_ref[...] * inv
    target = target_ref[...]
    b_high, b_low = halves(target)
    b = jnp.concatenate([b_high, b_low], axis=1)
    both = jnp.concatenate([train.astype(BF16), cand.astype(BF16)], axis=1)
    folded = jnp.concatenate([train[:32].astype(BF16), train[32:].astype(BF16)], axis=1)
    for i in range(NQ):
        z_ref[i, 0:32, :] = folded
        z_ref[i, 32:48, :] = b
        y_ref[i, 0:64, :] = both
        y_ref[i, 64:80, :] = b
    side_ref[...] = jnp.concatenate(
        [target, jnp.broadcast_to(noise_ref[...], (RHS, S))], axis=1
    )


def row_side(y_ref, j, first):
    points = jnp.concatenate(
        [y_ref[2 * j, 0:64, first : first + 64], y_ref[2 * j + 1, 0:64, first : first + 64]],
        axis=1,
    ).astype(F32)
    norm = jnp.sum(points * points, axis=0, keepdims=True)
    extra = rows_of(128, [*thirds(norm), 1.0, 1.0, 1.0])
    return jnp.concatenate(
        [-2.0 * points, extra, jnp.zeros((48, 128), F32)], axis=0
    ).astype(BF16)


def col_side(z_ref, col_ref, b_ref):
    for z in range(NZ):
        low, high = z_ref[0, z].astype(F32), z_ref[1, z].astype(F32)
        first = jnp.concatenate([low[:, :64], high[:, :64]], axis=1)
        second = jnp.concatenate([low[:, 64:], high[:, 64:]], axis=1)
        points = jnp.concatenate([first[0:32], second[0:32]], axis=0)
        b_ref[:, z * 128 : z * 128 + 128] = jnp.concatenate(
            [first[32:48], second[32:48]], axis=0
        ).astype(BF16)
        norm = jnp.sum(points * points, axis=0, keepdims=True)
        extra = rows_of(128, [1.0, 1.0, 1.0, *thirds(norm)])
        full = jnp.concatenate([points, extra, jnp.zeros((48, 128), F32)], axis=0)
        col_ref[z * 128 : z * 128 + 128, :] = full.T.astype(BF16)


def matern_of(inner):
    five_dist = jnp.maximum(inner, 1e-30) * 5.0
    scaled = five_dist * lax.rsqrt(five_dist)
    return (1.0 + scaled + five_dist * (1.0 / 3.0)) * jnp.exp2(scaled * (-LOG2E))


def piece(tile_ref, hbm_ref, sems, i):
    span = pl.ds(pl.multiple_of(i * PIECE, PIECE), PIECE)
    return tile_ref.at[span, :], hbm_ref.at[span, :], sems.at[i]


def fill(col_ref, row_ref, kern_ref, even_ref, odd_ref, send=None, low_ref=None):
    def inner(z, out_ref):
        points = col_ref[pl.ds(pl.multiple_of(z * 128, 128), 128), :]
        out_ref[...] = jnp.dot(points, row_ref[...], preferred_element_type=F32)

    def spread(z, in_ref):
        for i in range(8):
            span = pl.ds(pl.multiple_of(z * 128 + i * 16, 16), 16)
            kern = matern_of(in_ref[i * 16 : i * 16 + 16, :])
            high, low = halves(kern)
            kern_ref[span, :] = high
            if low_ref is not None:
                low_ref[span, :] = low

    inner(0, even_ref)

    def step(i, _):
        if send is not None:
            pl.when(i > 0)(lambda: send(i - 1))
        inner(2 * i + 1, odd_ref)
        spread(2 * i, even_ref)
        inner(jnp.minimum(2 * i + 2, NZ - 1), even_ref)
        spread(2 * i + 1, odd_ref)
        return 0

    lax.fori_loop(0, NZ // 2, step, 0)


def finish_fill(vectors_ref, kern_ref, hbm_ref, sems):
    total = None
    for i in range(CHUNKS):
        span = slice(i * PIECE, i * PIECE + PIECE)
        part = jnp.dot(vectors_ref[:, span], kern_ref[span, :], preferred_element_type=F32)
        total = part if total is None else total + part
        if i == 0:
            pltpu.make_async_copy(*piece(kern_ref, hbm_ref, sems, CHUNKS - 1)).start()
    return total[0:16] + total[16:32]


def drain(kern_ref, hbm_ref, sems):
    for i in range(CHUNKS):
        pltpu.make_async_copy(*piece(kern_ref, hbm_ref, sems, i)).wait()


def own_block(q):
    return pl.ds(pl.multiple_of((q // 2) * 128, 128), 128)


def own_mask(q):
    lane = lax.broadcasted_iota(jnp.int32, (RHS, 128), 1)
    return (lane // 64) == (q % 2)


def position():
    return lax.axis_index("y") * 4 + lax.axis_index("x")


def first_apply(
    y_ref, col_ref, b_ref, side_ref, hbm_ref, out_ref,
    acc_ref, row_ref, even_ref, odd_ref, kern_ref, sems,
):
    q = position()
    for j in range(NQ // 2):
        row_ref[:, j * 128 : j * 128 + 128] = row_side(y_ref, j, 0)

    def send(i):
        pltpu.make_async_copy(*piece(kern_ref, hbm_ref, sems, i)).start()

    fill(col_ref, row_ref, kern_ref, even_ref, odd_ref, send)
    acc_ref[...] = finish_fill(b_ref, kern_ref, hbm_ref, sems)
    own = side_ref[:, 0:64] * side_ref[:, 64:128]
    twice = jnp.concatenate([own, own], axis=1)
    acc_ref[:, own_block(q)] += jnp.where(own_mask(q), twice, 0.0)
    image = acc_ref[...].astype(BF16)
    for i in range(NQ):
        out_ref[i] = image
    drain(kern_ref, hbm_ref, sems)


def merge_image(part_ref, y_ref, out_ref, w_ref, br_ref):
    q = position()
    total = part_ref[0].astype(F32)
    for i in range(1, NQ):
        total = total + part_ref[i].astype(F32)
    w_ref[...] = total
    for j in range(NQ // 2):
        even, odd = y_ref[2 * j, 64:80, :].astype(F32), y_ref[2 * j + 1, 64:80, :].astype(F32)
        br_ref[:, j * 128 : j * 128 + 128] = jnp.concatenate(
            [even[:, :64] + even[:, 64:], odd[:, :64] + odd[:, 64:]], axis=1
        )
    b = br_ref[...]
    bw = jnp.sum(b * total, axis=1, keepdims=True)
    bb = jnp.sum(b * b, axis=1, keepdims=True)
    block = w_ref[:, own_block(q)]
    own = jnp.where(q % 2 == 0, block[:, :64], block[:, 64:])
    lane = lax.broadcasted_iota(jnp.int32, (RHS, 64), 1)
    scalars = jnp.zeros((RHS, 64), F32)
    for i, piece in enumerate([*thirds(bw), *thirds(bb)]):
        scalars = jnp.where(lane == i, piece, scalars)
    message = jnp.concatenate([own, scalars], axis=1).astype(BF16)
    for i in range(NZ):
        out_ref[i] = message


def fetch(hbm_ref, tile_ref, sems, i):
    target, source, sem = piece(tile_ref, hbm_ref, sems, i)
    return pltpu.make_async_copy(source, target, sem)


def streamed(r_ref, hbm_ref, tile_ref, sems):
    total = None
    for i in range(CHUNKS):
        fetch(hbm_ref, tile_ref, sems, i).wait()
        span = slice(i * PIECE, i * PIECE + PIECE)
        part = jnp.dot(r_ref[:, span], tile_ref[span, :], preferred_element_type=F32)
        total = part if total is None else total + part
    return total[0:16] + total[16:32]


def second_apply(
    s_ref, b_ref, w_ref, br_ref, kern_hbm, side_ref, out_ref, r_ref, own_ref, kern_ref, sems
):
    for i in range(CHUNKS):
        fetch(kern_hbm, kern_ref, sems, i).start()
    q = position()
    sums = s_ref[0, 0, :, 64:128].astype(F32)
    for c in range(2):
        for z in range(NZ):
            if c or z:
                sums = sums + s_ref[c, z, :, 64:128].astype(F32)
    lane = lax.broadcasted_iota(jnp.int32, (RHS, 64), 1)
    bw = jnp.sum(jnp.where(lane < 3, sums, 0.0), axis=1, keepdims=True)
    bb = jnp.sum(jnp.where((lane >= 3) & (lane < 6), sums, 0.0), axis=1, keepdims=True)
    alpha = bb / bw
    for z in range(NZ):
        span = slice(z * 128, z * 128 + 128)
        w = jnp.concatenate([s_ref[0, z, :, 0:64], s_ref[1, z, :, 0:64]], axis=1).astype(F32)
        b = b_ref[0:16, span].astype(F32) + b_ref[16:32, span].astype(F32)
        high, low = halves(b - alpha * w)
        r_ref[:, span] = jnp.concatenate([high, low], axis=0)
    r_row = br_ref[...] - alpha * w_ref[...]
    block = w_ref[:, own_block(q)]
    own_w = jnp.where(q % 2 == 0, block[:, :64], block[:, 64:])
    target, noise = side_ref[:, 0:64], side_ref[:, 64:128]
    own_r = target - alpha * own_w
    t = jnp.sum(own_r * own_w, axis=1, keepdims=True)
    rr = jnp.sum(own_r * own_r, axis=1, keepdims=True)
    side = jnp.where(lane == 0, bb, jnp.where(lane == 1, bw, 0.0))
    own_ref[...] = jnp.concatenate([own_r, side], axis=1)
    applied = streamed(r_ref, kern_hbm, kern_ref, sems)
    s = jnp.sum(r_row * applied, axis=1, keepdims=True) + jnp.sum(
        noise * own_r * own_r, axis=1, keepdims=True
    )
    wide = lax.broadcasted_iota(jnp.int32, (RHS, 128), 1)
    index = lax.broadcasted_iota(jnp.int32, (RHS, 128), 0)
    spread = (
        jnp.where(wide == index, s, 0.0)
        + jnp.where(wide == index + 16, t, 0.0)
        + jnp.where(wide == index + 32, rr, 0.0)
    )
    spread = jnp.sum(spread, axis=0, keepdims=True)
    for i in range(NZ):
        out_ref[i] = spread


def cand_mean(
    y_ref, col_ref, b_ref, r_ref, out_ref, row_ref, even_ref, odd_ref, kern_ref, low_ref
):
    for j in range(NQ // 2):
        row_ref[:, j * 128 : j * 128 + 128] = row_side(y_ref, j, 64)
    fill(col_ref, row_ref, kern_ref, even_ref, odd_ref, low_ref=low_ref)
    vectors = jnp.concatenate([b_ref[...], r_ref[...]], axis=0)
    total = jnp.dot(vectors, kern_ref[...], preferred_element_type=F32) + jnp.dot(
        vectors, low_ref[...], preferred_element_type=F32
    )
    mean0, mean = total[0:16] + total[16:32], total[32:48] + total[48:64]
    for i in range(NQ):
        span = slice(i * 64, i * 64 + 64)
        out_ref[i] = jnp.concatenate([mean0[:, span], mean[:, span]], axis=1)


def pack(s_ref, mean_ref, out_ref):
    total = s_ref[0, 0]
    for c in range(2):
        for z in range(NZ):
            if c or z:
                total = total + s_ref[c, z]
    eight = lax.broadcasted_iota(jnp.int32, (8, 128), 0)
    total = jnp.where(eight == 0, total, 0.0)
    for i in range(NQ):
        out_ref[i, 0:16, :] = mean_ref[i]
        out_ref[i, 16:24, :] = total


def finish(part_ref, own_ref, side_ref, solution_ref, post_ref):
    total = part_ref[0]
    for i in range(1, NQ):
        total = total + part_ref[i]
    mean, scalars = total[0:16], total[16:17]
    s, t, rr = column(scalars, 0), column(scalars, 16), column(scalars, 32)
    own_r = own_ref[:, 0:64]
    bb, bw = own_ref[:, 64:65], own_ref[:, 65:66]
    alpha0 = bb / bw
    beta = rr / bb
    alpha1 = rr / (s + 2.0 * beta * t + beta * beta * bw)
    target = side_ref[:, 0:64]
    solution_ref[...] = alpha0 * target + alpha1 * (own_r + beta * target)
    post_ref[...] = (alpha0 + alpha1 * beta) * mean[:, :64] + alpha1 * mean[:, 64:]


def shape(*dims, dtype=F32):
    return jax.ShapeDtypeStruct(dims, dtype)


def in_hbm(array):
    return pltpu.with_memory_space_constraint(array, pltpu.HBM)


def per_device(train_points, cand_points, inv_length, noise, targets):
    def call(kernel, **options):
        return pl.pallas_call(kernel, compiler_params=PARAMS, **options)

    vmem = pl.BlockSpec(memory_space=pltpu.VMEM)
    hbm = pl.BlockSpec(memory_space=pltpu.HBM)
    whole_tile = [pltpu.VMEM((COLS, ROWS), BF16), pltpu.SemaphoreType.DMA((CHUNKS,))]
    build = [
        pltpu.VMEM((128, ROWS), BF16),
        pltpu.VMEM((128, ROWS), F32),
        pltpu.VMEM((128, ROWS), F32),
    ]
    build_cost = pl.CostEstimate(
        flops=2 * ROWS * COLS * 160, bytes_accessed=2 * ROWS * COLS, transcendentals=2 * ROWS * COLS
    )

    y_out, z_out, side = call(
        prepare,
        in_specs=[hbm] * 5,
        out_shape=(
            shape(NQ, 80, 128, dtype=BF16),
            shape(NZ, 48, 128, dtype=BF16),
            shape(RHS, 128),
        ),
        scratch_shapes=[
            pltpu.VMEM((D, S), F32),
            pltpu.VMEM((D, S), F32),
            pltpu.VMEM((1, D), F32),
            pltpu.VMEM((1, S), F32),
            pltpu.VMEM((RHS, S), F32),
            pltpu.SemaphoreType.DMA((5,)),
        ],
    )(
        in_hbm(train_points),
        in_hbm(cand_points),
        in_hbm(inv_length.reshape(1, D)),
        in_hbm(noise.reshape(1, S)),
        in_hbm(targets),
    )
    z_in = lax.all_gather(lax.all_to_all(z_out, "z", 0, 0), "c", axis=0)
    y_in = lax.all_to_all(y_out, ("y", "x"), 0, 0)
    col, b_col = call(
        col_side,
        out_shape=(shape(COLS, 128, dtype=BF16), shape(32, COLS, dtype=BF16)),
        cost_estimate=pl.CostEstimate(
            flops=COLS * 1000, bytes_accessed=4 * COLS * 128, transcendentals=0
        ),
    )(z_in)
    kern, image_out = call(
        first_apply,
        out_specs=(hbm, vmem),
        out_shape=(pltpu.HBM((COLS, ROWS), BF16), shape(NQ, RHS, ROWS, dtype=BF16)),
        scratch_shapes=[pltpu.VMEM((RHS, ROWS), F32), *build, *whole_tile],
        cost_estimate=build_cost,
    )(y_in, col, b_col, side)
    image_in = lax.all_to_all(image_out, ("y", "x"), 0, 0)
    w_out, w_row, b_row = call(
        merge_image,
        out_shape=(shape(NZ, RHS, 128, dtype=BF16), shape(RHS, ROWS), shape(RHS, ROWS)),
    )(image_in, y_in)
    w_in = lax.all_gather(lax.all_to_all(w_out, "z", 0, 0), "c", axis=0)
    scalar_out, r_col, own = call(
        second_apply,
        in_specs=[vmem] * 4 + [hbm, vmem],
        out_shape=(shape(NZ, 1, 128), shape(32, COLS, dtype=BF16), shape(RHS, 128)),
        scratch_shapes=whole_tile,
    )(w_in, b_col, w_row, b_row, in_hbm(kern), side)
    scalar_in = lax.all_gather(lax.all_to_all(scalar_out, "z", 0, 0), "c", axis=0)
    mean_part = call(
        cand_mean,
        out_shape=shape(NQ, RHS, 128),
        scratch_shapes=[*build, *[pltpu.VMEM((COLS, ROWS), BF16)] * 2],
        cost_estimate=build_cost,
    )(y_in, col, b_col, r_col)
    mean_out = call(pack, out_shape=shape(NQ, 24, 128))(scalar_in, mean_part)
    mean_in = lax.all_to_all(mean_out, ("y", "x"), 0, 0)
    return call(finish, out_shape=(shape(RHS, S), shape(RHS, S)))(mean_in, own, side)


def solution(mesh):
    fine = Mesh(mesh.devices.reshape(16, 2, 4, 4), ("z", "c", "y", "x"))
    every = ("z", "c", "y", "x")
    wide = P(None, every)
    return jax.shard_map(
        per_device,
        mesh=fine,
        in_specs=(wide, wide, P(), P(every), wide),
        out_specs=(wide, wide),
        check_vma=False,
    )
```

```python
import math

import jax
import jax.numpy as jnp
from jax import lax
from jax.experimental import pallas as pl
from jax.experimental.pallas import tpu as pltpu
from jax.sharding import Mesh, PartitionSpec as P

F32 = jnp.float32
BF16 = jnp.bfloat16

D = 64
S = 64
RHS = 16
NQ = 16
NZ = 16
ROWS = NQ * S
COLS = 2 * NZ * S
LOG2E = math.log2(math.e)
CHUNKS = 8
PIECE = COLS // CHUNKS
KEPT = 2
PARAMS = pltpu.CompilerParams(vmem_limit_bytes=24 * 1024 * 1024)


def halves(value):
    high = value.astype(BF16)
    return high, (value - high.astype(F32)).astype(BF16)


def thirds(value):
    high = value.astype(BF16).astype(F32)
    rest = value - high
    middle = rest.astype(BF16).astype(F32)
    low = (rest - middle).astype(BF16).astype(F32)
    return high, middle, low


def rows_of(width, pieces):
    index = lax.broadcasted_iota(jnp.int32, (16, width), 0)
    total = jnp.zeros((16, width), F32)
    for i, piece in enumerate(pieces):
        total = jnp.where(index == i, piece, total)
    return total


def column(row, start):
    lane = lax.broadcasted_iota(jnp.int32, (RHS, 128), 1)
    index = lax.broadcasted_iota(jnp.int32, (RHS, 128), 0)
    return jnp.sum(jnp.where(lane == index + start, row, 0.0), axis=1, keepdims=True)


def load(pairs, sems):
    copies = [
        pltpu.make_async_copy(source, target, sems.at[i])
        for i, (source, target) in enumerate(pairs)
    ]
    for copy in copies:
        copy.start()
    for copy in copies:
        copy.wait()


def scale_column(inv_ref):
    eye = lax.broadcasted_iota(jnp.int32, (D, D), 0) == lax.broadcasted_iota(
        jnp.int32, (D, D), 1
    )
    return jnp.sum(jnp.where(eye, inv_ref[...], 0.0), axis=1, keepdims=True)


def prepare_z(
    train_hbm, inv_hbm, target_hbm, z_ref, scaled_ref, inv_ref, b_ref, train_ref, target_ref, sems
):
    load([(train_hbm, train_ref), (inv_hbm, inv_ref), (target_hbm, target_ref)], sems)
    train = train_ref[...] * scale_column(inv_ref)
    scaled_ref[...] = train.astype(BF16)
    b = jnp.concatenate(halves(target_ref[...]), axis=1)
    b_ref[...] = b
    folded = jnp.concatenate([train[:32].astype(BF16), train[32:].astype(BF16)], axis=1)
    for i in range(NZ):
        z_ref[i, 0:32, :] = folded
        z_ref[i, 32:48, :] = b


def prepare_y(
    cand_hbm, noise_hbm, target_hbm, scaled_ref, inv_ref, b_ref, y_ref, side_ref,
    cand_ref, noise_ref, target_ref, sems,
):
    load([(cand_hbm, cand_ref), (noise_hbm, noise_ref), (target_hbm, target_ref)], sems)
    cand = (cand_ref[...] * scale_column(inv_ref)).astype(BF16)
    both = jnp.concatenate([scaled_ref[...], cand], axis=1)
    b = b_ref[...]
    for i in range(NQ):
        y_ref[i, 0:64, :] = both
        y_ref[i, 64:80, :] = b
    side_ref[...] = jnp.concatenate(
        [target_ref[...], jnp.broadcast_to(noise_ref[...], (RHS, S))], axis=1
    )


def row_side(y_ref, j, first):
    points = jnp.concatenate(
        [y_ref[2 * j, 0:64, first : first + 64], y_ref[2 * j + 1, 0:64, first : first + 64]],
        axis=1,
    ).astype(F32)
    norm = jnp.sum(points * points, axis=0, keepdims=True)
    extra = rows_of(128, [*thirds(norm), 1.0, 1.0, 1.0])
    return jnp.concatenate(
        [-2.0 * points, extra, jnp.zeros((48, 128), F32)], axis=0
    ).astype(BF16)


def col_side(z_ref, col_ref, b_ref):
    for z in range(NZ):
        low, high = z_ref[0, z].astype(F32), z_ref[1, z].astype(F32)
        first = jnp.concatenate([low[:, :64], high[:, :64]], axis=1)
        second = jnp.concatenate([low[:, 64:], high[:, 64:]], axis=1)
        points = jnp.concatenate([first[0:32], second[0:32]], axis=0)
        b_ref[:, z * 128 : z * 128 + 128] = jnp.concatenate(
            [first[32:48], second[32:48]], axis=0
        ).astype(BF16)
        norm = jnp.sum(points * points, axis=0, keepdims=True)
        extra = rows_of(128, [1.0, 1.0, 1.0, *thirds(norm)])
        full = jnp.concatenate([points, extra, jnp.zeros((48, 128), F32)], axis=0)
        col_ref[z * 128 : z * 128 + 128, :] = full.T.astype(BF16)


def matern_of(inner):
    five_dist = jnp.maximum(inner, 1e-30) * 5.0
    scaled = five_dist * lax.rsqrt(five_dist)
    return (1.0 + scaled + five_dist * (1.0 / 3.0)) * jnp.exp2(scaled * (-LOG2E))


def piece(tile_ref, hbm_ref, sems, i):
    span = pl.ds(pl.multiple_of(i * PIECE, PIECE), PIECE)
    return tile_ref.at[span, :], hbm_ref.at[span, :], sems.at[i]


def fill(col_ref, row_ref, kern_ref, even_ref, odd_ref, send, stored, low_ref=None):
    def inner(z, out_ref):
        points = col_ref[pl.ds(pl.multiple_of(z * 128, 128), 128), :]
        out_ref[...] = jnp.dot(points, row_ref[...], preferred_element_type=F32)

    def spread(z, in_ref):
        for i in range(8):
            span = pl.ds(pl.multiple_of(z * 128 + i * 16, 16), 16)
            kern = matern_of(in_ref[i * 16 : i * 16 + 16, :])
            high, low = halves(kern)
            kern_ref[span, :] = high
            if low_ref is not None:
                low_ref[span, :] = low

    inner(0, even_ref)

    def step(i, _):
        pl.when((i > 0) & (i <= stored))(lambda: send(i - 1))
        inner(2 * i + 1, odd_ref)
        spread(2 * i, even_ref)
        inner(jnp.minimum(2 * i + 2, NZ - 1), even_ref)
        spread(2 * i + 1, odd_ref)
        return 0

    lax.fori_loop(0, NZ // 2, step, 0)


def sender(kern_ref, hbm_ref, sems):
    def send(i):
        pltpu.make_async_copy(*piece(kern_ref, hbm_ref, sems, i)).start()

    return send


def drain(kern_ref, hbm_ref, sems, stored):
    for i in range(stored):
        pltpu.make_async_copy(*piece(kern_ref, hbm_ref, sems, i)).wait()


def own_block(q):
    return pl.ds(pl.multiple_of((q // 2) * 128, 128), 128)


def own_mask(q):
    lane = lax.broadcasted_iota(jnp.int32, (RHS, 128), 1)
    return (lane // 64) == (q % 2)


def position():
    return lax.axis_index("y") * 4 + lax.axis_index("x")


def first_apply(
    y_ref, col_ref, b_ref, side_ref, hbm_ref, kept_ref, out_ref,
    acc_ref, row_ref, even_ref, odd_ref, kern_ref, sems,
):
    q = position()
    stored = CHUNKS - KEPT
    for j in range(NQ // 2):
        row_ref[:, j * 128 : j * 128 + 128] = row_side(y_ref, j, 0)
    send = sender(kern_ref, hbm_ref, sems)
    fill(col_ref, row_ref, kern_ref, even_ref, odd_ref, send, stored)
    total = jnp.dot(b_ref[...], kern_ref[...], preferred_element_type=F32)
    acc_ref[...] = total[0:16] + total[16:32]
    kept_ref[...] = kern_ref[stored * PIECE :, :]
    own = side_ref[:, 0:64] * side_ref[:, 64:128]
    twice = jnp.concatenate([own, own], axis=1)
    acc_ref[:, own_block(q)] += jnp.where(own_mask(q), twice, 0.0)
    image = acc_ref[...].astype(BF16)
    for i in range(NQ):
        out_ref[i] = image
    drain(kern_ref, hbm_ref, sems, stored)


def cand_apply(
    y_ref, col_ref, b_ref, hbm_ref, mean_ref, row_ref, even_ref, odd_ref, low_ref, kern_ref, sems
):
    for j in range(NQ // 2):
        row_ref[:, j * 128 : j * 128 + 128] = row_side(y_ref, j, 64)
    send = sender(kern_ref, hbm_ref, sems)
    fill(col_ref, row_ref, kern_ref, even_ref, odd_ref, send, CHUNKS, low_ref)
    total = jnp.dot(b_ref[...], low_ref[...], preferred_element_type=F32)
    send(CHUNKS - 1)
    total = total + jnp.dot(b_ref[...], kern_ref[...], preferred_element_type=F32)
    mean_ref[...] = total[0:16] + total[16:32]
    drain(kern_ref, hbm_ref, sems, CHUNKS)


def merge_image(part_ref, y_ref, out_ref, w_ref, br_ref):
    q = position()
    total = part_ref[0].astype(F32)
    for i in range(1, NQ):
        total = total + part_ref[i].astype(F32)
    w_ref[...] = total
    for j in range(NQ // 2):
        even, odd = y_ref[2 * j, 64:80, :].astype(F32), y_ref[2 * j + 1, 64:80, :].astype(F32)
        br_ref[:, j * 128 : j * 128 + 128] = jnp.concatenate(
            [even[:, :64] + even[:, 64:], odd[:, :64] + odd[:, 64:]], axis=1
        )
    b = br_ref[...]
    bw = jnp.sum(b * total, axis=1, keepdims=True)
    bb = jnp.sum(b * b, axis=1, keepdims=True)
    block = w_ref[:, own_block(q)]
    own = jnp.where(q % 2 == 0, block[:, :64], block[:, 64:])
    lane = lax.broadcasted_iota(jnp.int32, (RHS, 64), 1)
    scalars = jnp.zeros((RHS, 64), F32)
    for i, piece in enumerate([*thirds(bw), *thirds(bb)]):
        scalars = jnp.where(lane == i, piece, scalars)
    message = jnp.concatenate([own, scalars], axis=1).astype(BF16)
    for i in range(NZ):
        out_ref[i] = message


def fetch(hbm_ref, tile_ref, sems, i):
    target, source, sem = piece(tile_ref, hbm_ref, sems, i)
    return pltpu.make_async_copy(source, target, sem)


def streamed(r_ref, hbm_ref, tile_ref, sems, stored, kept_ref=None):
    total = jnp.zeros((32, ROWS), F32)
    if kept_ref is not None:
        total = jnp.dot(r_ref[:, stored * PIECE :], kept_ref[...], preferred_element_type=F32)
    for i in range(stored):
        fetch(hbm_ref, tile_ref, sems, i).wait()
        span = slice(i * PIECE, i * PIECE + PIECE)
        total = total + jnp.dot(r_ref[:, span], tile_ref[span, :], preferred_element_type=F32)
    return total[0:16] + total[16:32]


def second_apply(
    s_ref, b_ref, w_ref, br_ref, kern_hbm, kept_ref, side_ref, mean_ref,
    out_ref, r_ref, own_ref, kern_ref, sems,
):
    stored = CHUNKS - KEPT
    for i in range(stored):
        fetch(kern_hbm, kern_ref, sems, i).start()
    q = position()
    sums = s_ref[0, 0, :, 64:128].astype(F32)
    for c in range(2):
        for z in range(NZ):
            if c or z:
                sums = sums + s_ref[c, z, :, 64:128].astype(F32)
    lane = lax.broadcasted_iota(jnp.int32, (RHS, 64), 1)
    bw = jnp.sum(jnp.where(lane < 3, sums, 0.0), axis=1, keepdims=True)
    bb = jnp.sum(jnp.where((lane >= 3) & (lane < 6), sums, 0.0), axis=1, keepdims=True)
    alpha = bb / bw
    for z in range(NZ):
        span = slice(z * 128, z * 128 + 128)
        w = jnp.concatenate([s_ref[0, z, :, 0:64], s_ref[1, z, :, 0:64]], axis=1).astype(F32)
        b = b_ref[0:16, span].astype(F32) + b_ref[16:32, span].astype(F32)
        high, low = halves(b - alpha * w)
        r_ref[:, span] = jnp.concatenate([high, low], axis=0)
    r_row = br_ref[...] - alpha * w_ref[...]
    block = w_ref[:, own_block(q)]
    own_w = jnp.where(q % 2 == 0, block[:, :64], block[:, 64:])
    target, noise = side_ref[:, 0:64], side_ref[:, 64:128]
    own_r = target - alpha * own_w
    t = jnp.sum(own_r * own_w, axis=1, keepdims=True)
    rr = jnp.sum(own_r * own_r, axis=1, keepdims=True)
    side = jnp.where(lane == 0, bb, jnp.where(lane == 1, bw, 0.0))
    own_ref[...] = jnp.concatenate([own_r, side], axis=1)
    applied = streamed(r_ref, kern_hbm, kern_ref, sems, stored, kept_ref)
    s = jnp.sum(r_row * applied, axis=1, keepdims=True) + jnp.sum(
        noise * own_r * own_r, axis=1, keepdims=True
    )
    wide = lax.broadcasted_iota(jnp.int32, (RHS, 128), 1)
    index = lax.broadcasted_iota(jnp.int32, (RHS, 128), 0)
    spread = (
        jnp.where(wide == index, s, 0.0)
        + jnp.where(wide == index + 16, t, 0.0)
        + jnp.where(wide == index + 32, rr, 0.0)
    )
    spread = jnp.sum(spread, axis=0, keepdims=True)
    for i in range(2 * NZ):
        out_ref[i] = spread


def cand_mean(r_ref, cand_hbm, mean_ref, out_ref, cand_ref, sems):
    for i in range(CHUNKS):
        fetch(cand_hbm, cand_ref, sems, i).start()
    mean0 = mean_ref[...]
    mean = streamed(r_ref, cand_hbm, cand_ref, sems, CHUNKS)
    for i in range(NQ):
        span = slice(i * 64, i * 64 + 64)
        out_ref[i] = jnp.concatenate([mean0[:, span], mean[:, span]], axis=1)


def pack(s_ref, mean_ref, out_ref):
    total = s_ref[0]
    for i in range(1, 2 * NZ):
        total = total + s_ref[i]
    eight = lax.broadcasted_iota(jnp.int32, (8, 128), 0)
    total = jnp.where(eight == 0, total, 0.0)
    for i in range(NQ):
        out_ref[i, 0:16, :] = mean_ref[i]
        out_ref[i, 16:24, :] = total


def finish(part_ref, own_ref, side_ref, solution_ref, post_ref):
    total = part_ref[0]
    for i in range(1, NQ):
        total = total + part_ref[i]
    mean, scalars = total[0:16], total[16:17]
    s, t, rr = column(scalars, 0), column(scalars, 16), column(scalars, 32)
    own_r = own_ref[:, 0:64]
    bb, bw = own_ref[:, 64:65], own_ref[:, 65:66]
    alpha0 = bb / bw
    beta = rr / bb
    alpha1 = rr / (s + 2.0 * beta * t + beta * beta * bw)
    target = side_ref[:, 0:64]
    solution_ref[...] = alpha0 * target + alpha1 * (own_r + beta * target)
    post_ref[...] = (alpha0 + alpha1 * beta) * mean[:, :64] + alpha1 * mean[:, 64:]


def shape(*dims, dtype=F32):
    return jax.ShapeDtypeStruct(dims, dtype)


def in_hbm(array):
    return pltpu.with_memory_space_constraint(array, pltpu.HBM)


def per_device(train_points, cand_points, inv_length, noise, targets):
    def call(kernel, **options):
        return pl.pallas_call(kernel, compiler_params=PARAMS, **options)

    vmem = pl.BlockSpec(memory_space=pltpu.VMEM)
    hbm = pl.BlockSpec(memory_space=pltpu.HBM)
    whole_tile = [pltpu.VMEM((COLS, ROWS), BF16), pltpu.SemaphoreType.DMA((CHUNKS,))]
    build = [
        pltpu.VMEM((128, ROWS), BF16),
        pltpu.VMEM((128, ROWS), F32),
        pltpu.VMEM((128, ROWS), F32),
    ]
    build_cost = pl.CostEstimate(
        flops=2 * ROWS * COLS * 160, bytes_accessed=2 * ROWS * COLS, transcendentals=2 * ROWS * COLS
    )

    points = pltpu.VMEM((D, S), F32)
    row = pltpu.VMEM((1, S), F32)
    rows = pltpu.VMEM((RHS, S), F32)
    three = pltpu.SemaphoreType.DMA((3,))
    inv_length, noise = inv_length.reshape(1, D), noise.reshape(1, S)
    z_out, scaled, inv, b = call(
        prepare_z,
        in_specs=[hbm] * 3,
        out_shape=(
            shape(NZ, 48, 128, dtype=BF16),
            shape(D, S, dtype=BF16),
            shape(1, D),
            shape(RHS, 128, dtype=BF16),
        ),
        scratch_shapes=[points, rows, three],
    )(in_hbm(train_points), in_hbm(inv_length), in_hbm(targets))
    z_in = lax.all_gather(lax.all_to_all(z_out, "z", 0, 0), "c", axis=0)
    y_out, side = call(
        prepare_y,
        in_specs=[hbm] * 3 + [vmem] * 3,
        out_shape=(shape(NQ, 80, 128, dtype=BF16), shape(RHS, 128)),
        scratch_shapes=[points, row, rows, three],
        cost_estimate=pl.CostEstimate(flops=100000, bytes_accessed=500000, transcendentals=0),
    )(in_hbm(cand_points), in_hbm(noise), in_hbm(targets), scaled, inv, b)
    y_in = lax.all_to_all(y_out, ("y", "x"), 0, 0)
    col, b_col = call(
        col_side,
        out_shape=(shape(COLS, 128, dtype=BF16), shape(32, COLS, dtype=BF16)),
        cost_estimate=pl.CostEstimate(
            flops=COLS * 1000, bytes_accessed=4 * COLS * 128, transcendentals=0
        ),
    )(z_in)
    stored = (CHUNKS - KEPT) * PIECE
    kern, kept, image_out = call(
        first_apply,
        out_specs=(hbm, vmem, vmem),
        out_shape=(
            pltpu.HBM((stored, ROWS), BF16),
            shape(COLS - stored, ROWS, dtype=BF16),
            shape(NQ, RHS, ROWS, dtype=BF16),
        ),
        scratch_shapes=[pltpu.VMEM((RHS, ROWS), F32), *build, *whole_tile],
        cost_estimate=build_cost,
    )(y_in, col, b_col, side)
    image_in = lax.all_to_all(image_out, ("y", "x"), 0, 0)
    kern_cand, mean0 = call(
        cand_apply,
        out_specs=(hbm, vmem),
        out_shape=(pltpu.HBM((COLS, ROWS), BF16), shape(RHS, ROWS)),
        scratch_shapes=[*build, pltpu.VMEM((COLS, ROWS), BF16), *whole_tile],
        cost_estimate=build_cost,
    )(y_in, col, b_col)
    w_out, w_row, b_row = call(
        merge_image,
        out_shape=(shape(NZ, RHS, 128, dtype=BF16), shape(RHS, ROWS), shape(RHS, ROWS)),
    )(image_in, y_in)
    w_in = lax.all_gather(lax.all_to_all(w_out, "z", 0, 0), "c", axis=0)
    scalar_out, r_col, own = call(
        second_apply,
        in_specs=[vmem] * 4 + [hbm] + [vmem] * 3,
        out_shape=(shape(2 * NZ, 1, 128), shape(32, COLS, dtype=BF16), shape(RHS, 128)),
        scratch_shapes=[pltpu.VMEM((stored, ROWS), BF16), pltpu.SemaphoreType.DMA((CHUNKS,))],
    )(w_in, b_col, w_row, b_row, in_hbm(kern), kept, side, mean0)
    scalar_in = lax.all_to_all(scalar_out, ("z", "c"), 0, 0)
    mean_part = call(
        cand_mean,
        in_specs=[vmem, hbm, vmem],
        out_shape=shape(NQ, RHS, 128),
        scratch_shapes=whole_tile,
        cost_estimate=pl.CostEstimate(
            flops=2 * ROWS * COLS * 32, bytes_accessed=2 * ROWS * COLS, transcendentals=0
        ),
    )(r_col, in_hbm(kern_cand), mean0)
    mean_out = call(pack, out_shape=shape(NQ, 24, 128))(scalar_in, mean_part)
    mean_in = lax.all_to_all(mean_out, ("y", "x"), 0, 0)
    return call(finish, out_shape=(shape(RHS, S), shape(RHS, S)))(mean_in, own, side)


def solution(mesh):
    fine = Mesh(mesh.devices.reshape(16, 2, 4, 4), ("z", "c", "y", "x"))
    every = ("z", "c", "y", "x")
    wide = P(None, every)
    return jax.shard_map(
        per_device,
        mesh=fine,
        in_specs=(wide, wide, P(), P(every), wide),
        out_specs=(wide, wide),
        check_vma=False,
    )
```

```python
import math

import jax
import jax.numpy as jnp
from jax import lax
from jax.experimental import pallas as pl
from jax.experimental.pallas import tpu as pltpu
from jax.sharding import Mesh, PartitionSpec as P

F32 = jnp.float32
BF16 = jnp.bfloat16

D = 64
S = 64
RHS = 16
NQ = 16
NZ = 16
ROWS = NQ * S
COLS = 2 * NZ * S
LOG2E = math.log2(math.e)
CHUNKS = 4
PIECE = COLS // CHUNKS
KEPT = 1
STORED = CHUNKS - KEPT
READ = 256
READS = STORED * PIECE // READ
PARAMS = pltpu.CompilerParams(vmem_limit_bytes=24 * 1024 * 1024)


def halves(value):
    high = value.astype(BF16)
    return high, (value - high.astype(F32)).astype(BF16)


def thirds(value):
    high = value.astype(BF16).astype(F32)
    rest = value - high
    middle = rest.astype(BF16).astype(F32)
    low = (rest - middle).astype(BF16).astype(F32)
    return high, middle, low


def rows_of(width, pieces):
    index = lax.broadcasted_iota(jnp.int32, (16, width), 0)
    total = jnp.zeros((16, width), F32)
    for i, piece in enumerate(pieces):
        total = jnp.where(index == i, piece, total)
    return total


def column(row, start):
    lane = lax.broadcasted_iota(jnp.int32, (RHS, 128), 1)
    index = lax.broadcasted_iota(jnp.int32, (RHS, 128), 0)
    return jnp.sum(jnp.where(lane == index + start, row, 0.0), axis=1, keepdims=True)


def prepare(
    train_hbm, cand_hbm, inv_hbm, noise_hbm, target_hbm, y_ref, z_ref, side_ref,
    train_ref, cand_ref, inv_ref, noise_ref, target_ref, sems,
):
    copies = [
        pltpu.make_async_copy(source, target, sems.at[i])
        for i, (source, target) in enumerate(
            [
                (train_hbm, train_ref),
                (inv_hbm, inv_ref),
                (target_hbm, target_ref),
                (cand_hbm, cand_ref),
                (noise_hbm, noise_ref),
            ]
        )
    ]
    for copy in copies:
        copy.start()
    for copy in copies:
        copy.wait()
    eye = lax.broadcasted_iota(jnp.int32, (D, D), 0) == lax.broadcasted_iota(
        jnp.int32, (D, D), 1
    )
    inv = jnp.sum(jnp.where(eye, inv_ref[...], 0.0), axis=1, keepdims=True)
    train = train_ref[...] * inv
    cand = cand_ref[...] * inv
    target = target_ref[...]
    b_high, b_low = halves(target)
    b = jnp.concatenate([b_high, b_low], axis=1)
    both = jnp.concatenate([train.astype(BF16), cand.astype(BF16)], axis=1)
    folded = jnp.concatenate([train[:32].astype(BF16), train[32:].astype(BF16)], axis=1)
    for i in range(NQ):
        z_ref[i, 0:32, :] = folded
        z_ref[i, 32:48, :] = b
        y_ref[i, 0:64, :] = both
        y_ref[i, 64:80, :] = b
    side_ref[...] = jnp.concatenate(
        [target, jnp.broadcast_to(noise_ref[...], (RHS, S))], axis=1
    )


def row_side(y_ref, j, first):
    points = jnp.concatenate(
        [y_ref[2 * j, 0:64, first : first + 64], y_ref[2 * j + 1, 0:64, first : first + 64]],
        axis=1,
    ).astype(F32)
    norm = jnp.sum(points * points, axis=0, keepdims=True)
    extra = rows_of(128, [*thirds(norm), 1.0, 1.0, 1.0])
    return jnp.concatenate(
        [-2.0 * points, extra, jnp.zeros((48, 128), F32)], axis=0
    ).astype(BF16)


def col_side(z_ref, col_ref, b_ref):
    for z in range(NZ):
        low, high = z_ref[0, z].astype(F32), z_ref[1, z].astype(F32)
        first = jnp.concatenate([low[:, :64], high[:, :64]], axis=1)
        second = jnp.concatenate([low[:, 64:], high[:, 64:]], axis=1)
        points = jnp.concatenate([first[0:32], second[0:32]], axis=0)
        b_ref[:, z * 128 : z * 128 + 128] = jnp.concatenate(
            [first[32:48], second[32:48]], axis=0
        ).astype(BF16)
        norm = jnp.sum(points * points, axis=0, keepdims=True)
        extra = rows_of(128, [1.0, 1.0, 1.0, *thirds(norm)])
        full = jnp.concatenate([points, extra, jnp.zeros((48, 128), F32)], axis=0)
        col_ref[z * 128 : z * 128 + 128, :] = full.T.astype(BF16)


def matern_of(inner):
    five_dist = jnp.maximum(inner, 1e-30) * 5.0
    scaled = five_dist * lax.rsqrt(five_dist)
    return (1.0 + scaled + five_dist * (1.0 / 3.0)) * jnp.exp2(scaled * (-LOG2E))


def piece(tile_ref, hbm_ref, sems, i):
    span = pl.ds(pl.multiple_of(i * PIECE, PIECE), PIECE)
    return tile_ref.at[span, :], hbm_ref.at[span, :], sems.at[i]


def fill(col_ref, row_ref, kern_ref, even_ref, odd_ref, before=None, low_ref=None):
    def inner(z, out_ref):
        points = col_ref[pl.ds(pl.multiple_of(z * 128, 128), 128), :]
        out_ref[...] = jnp.dot(points, row_ref[...], preferred_element_type=F32)

    def spread(z, in_ref):
        for i in range(8):
            span = pl.ds(pl.multiple_of(z * 128 + i * 16, 16), 16)
            kern = matern_of(in_ref[i * 16 : i * 16 + 16, :])
            if low_ref is None:
                kern_ref[span, :] = kern.astype(BF16)
            else:
                high, low = halves(kern)
                kern_ref[span, :] = high
                low_ref[span, :] = low

    def step(i, _):
        if before is not None:
            before(i)
        buffers = [even_ref, odd_ref]
        for k in range(4):
            z = 4 * i + k
            inner(jnp.minimum(z + 1, NZ - 1), buffers[(k + 1) % 2])
            spread(z, buffers[k % 2])
        return 0

    inner(0, even_ref)
    lax.fori_loop(0, NZ // 4, step, 0)


def own_block(q):
    return pl.ds(pl.multiple_of((q // 2) * 128, 128), 128)


def own_mask(q):
    lane = lax.broadcasted_iota(jnp.int32, (RHS, 128), 1)
    return (lane // 64) == (q % 2)


def position():
    return lax.axis_index("y") * 4 + lax.axis_index("x")


def first_apply(
    y_ref, col_ref, b_ref, side_ref, hbm_ref, kept_ref, out_ref,
    acc_ref, row_ref, even_ref, odd_ref, kern_ref, sems,
):
    q = position()
    for j in range(NQ // 2):
        row_ref[:, j * 128 : j * 128 + 128] = row_side(y_ref, j, 0)

    def before(i):
        @pl.when(i > 0)
        def _():
            pltpu.make_async_copy(*piece(kern_ref, hbm_ref, sems, i - 1)).start()

    fill(col_ref, row_ref, kern_ref, even_ref, odd_ref, before)
    total = jnp.dot(b_ref[...], kern_ref[...], preferred_element_type=F32)
    acc_ref[...] = total[0:16] + total[16:32]
    kept_ref[...] = kern_ref[STORED * PIECE :, :]
    own = side_ref[:, 0:64] * side_ref[:, 64:128]
    twice = jnp.concatenate([own, own], axis=1)
    acc_ref[:, own_block(q)] += jnp.where(own_mask(q), twice, 0.0)
    image = acc_ref[...].astype(BF16)
    for i in range(NQ):
        out_ref[i] = image
    for i in range(STORED):
        pltpu.make_async_copy(*piece(kern_ref, hbm_ref, sems, i)).wait()


def merge_image(part_ref, y_ref, out_ref, w_ref, br_ref):
    q = position()
    total = part_ref[0].astype(F32)
    for i in range(1, NQ):
        total = total + part_ref[i].astype(F32)
    w_ref[...] = total
    for j in range(NQ // 2):
        even, odd = y_ref[2 * j, 64:80, :].astype(F32), y_ref[2 * j + 1, 64:80, :].astype(F32)
        br_ref[:, j * 128 : j * 128 + 128] = jnp.concatenate(
            [even[:, :64] + even[:, 64:], odd[:, :64] + odd[:, 64:]], axis=1
        )
    b = br_ref[...]
    bw = jnp.sum(b * total, axis=1, keepdims=True)
    bb = jnp.sum(b * b, axis=1, keepdims=True)
    block = w_ref[:, own_block(q)]
    own = jnp.where(q % 2 == 0, block[:, :64], block[:, 64:])
    lane = lax.broadcasted_iota(jnp.int32, (RHS, 64), 1)
    scalars = jnp.zeros((RHS, 64), F32)
    for i, piece in enumerate([*thirds(bw), *thirds(bb)]):
        scalars = jnp.where(lane == i, piece, scalars)
    message = jnp.concatenate([own, scalars], axis=1).astype(BF16)
    for i in range(NZ):
        out_ref[i] = message


def fetch(hbm_ref, tile_ref, sems, i):
    span = slice(i * READ, i * READ + READ)
    return pltpu.make_async_copy(hbm_ref.at[span, :], tile_ref.at[span, :], sems.at[i])


def streamed(r_ref, hbm_ref, tile_ref, sems, kept_ref):
    total = jnp.dot(r_ref[:, STORED * PIECE :], kept_ref[...], preferred_element_type=F32)
    for i in range(READS):
        fetch(hbm_ref, tile_ref, sems, i).wait()
        span = slice(i * READ, i * READ + READ)
        total = total + jnp.dot(r_ref[:, span], tile_ref[span, :], preferred_element_type=F32)
    return total[0:16] + total[16:32]


def second_apply(
    s_ref, b_ref, w_ref, br_ref, kern_hbm, kept_ref, side_ref, out_ref, r_ref, own_ref,
    kern_ref, sems,
):
    for i in range(READS):
        fetch(kern_hbm, kern_ref, sems, i).start()
    q = position()
    sums = s_ref[0, 0, :, 64:128].astype(F32)
    for c in range(2):
        for z in range(NZ):
            if c or z:
                sums = sums + s_ref[c, z, :, 64:128].astype(F32)
    lane = lax.broadcasted_iota(jnp.int32, (RHS, 64), 1)
    bw = jnp.sum(jnp.where(lane < 3, sums, 0.0), axis=1, keepdims=True)
    bb = jnp.sum(jnp.where((lane >= 3) & (lane < 6), sums, 0.0), axis=1, keepdims=True)
    alpha = bb / bw
    for z in range(NZ):
        span = slice(z * 128, z * 128 + 128)
        w = jnp.concatenate([s_ref[0, z, :, 0:64], s_ref[1, z, :, 0:64]], axis=1).astype(F32)
        b = b_ref[0:16, span].astype(F32) + b_ref[16:32, span].astype(F32)
        high, low = halves(b - alpha * w)
        r_ref[:, span] = jnp.concatenate([high, low], axis=0)
    r_row = br_ref[...] - alpha * w_ref[...]
    block = w_ref[:, own_block(q)]
    own_w = jnp.where(q % 2 == 0, block[:, :64], block[:, 64:])
    target, noise = side_ref[:, 0:64], side_ref[:, 64:128]
    own_r = target - alpha * own_w
    t = jnp.sum(own_r * own_w, axis=1, keepdims=True)
    rr = jnp.sum(own_r * own_r, axis=1, keepdims=True)
    side = jnp.where(lane == 0, bb, jnp.where(lane == 1, bw, 0.0))
    own_ref[...] = jnp.concatenate([own_r, side], axis=1)
    applied = streamed(r_ref, kern_hbm, kern_ref, sems, kept_ref)
    s = jnp.sum(r_row * applied, axis=1, keepdims=True) + jnp.sum(
        noise * own_r * own_r, axis=1, keepdims=True
    )
    wide = lax.broadcasted_iota(jnp.int32, (RHS, 128), 1)
    index = lax.broadcasted_iota(jnp.int32, (RHS, 128), 0)
    spread = (
        jnp.where(wide == index, s, 0.0)
        + jnp.where(wide == index + 16, t, 0.0)
        + jnp.where(wide == index + 32, rr, 0.0)
    )
    spread = jnp.sum(spread, axis=0, keepdims=True)
    for i in range(NZ):
        out_ref[i] = spread


def cand_mean(
    y_ref, col_ref, b_ref, r_ref, out_ref, row_ref, even_ref, odd_ref, kern_ref, low_ref
):
    for j in range(NQ // 2):
        row_ref[:, j * 128 : j * 128 + 128] = row_side(y_ref, j, 64)
    fill(col_ref, row_ref, kern_ref, even_ref, odd_ref, low_ref=low_ref)
    vectors = jnp.concatenate([b_ref[...], r_ref[...]], axis=0)
    total = jnp.dot(vectors, kern_ref[...], preferred_element_type=F32) + jnp.dot(
        vectors, low_ref[...], preferred_element_type=F32
    )
    mean0, mean = total[0:16] + total[16:32], total[32:48] + total[48:64]
    for i in range(NQ):
        span = slice(i * 64, i * 64 + 64)
        out_ref[i] = jnp.concatenate([mean0[:, span], mean[:, span]], axis=1)


def pack(s_ref, mean_ref, out_ref):
    total = s_ref[0, 0]
    for c in range(2):
        for z in range(NZ):
            if c or z:
                total = total + s_ref[c, z]
    eight = lax.broadcasted_iota(jnp.int32, (8, 128), 0)
    total = jnp.where(eight == 0, total, 0.0)
    for i in range(NQ):
        out_ref[i, 0:16, :] = mean_ref[i]
        out_ref[i, 16:24, :] = total


def finish(part_ref, own_ref, side_ref, solution_ref, post_ref):
    total = part_ref[0]
    for i in range(1, NQ):
        total = total + part_ref[i]
    mean, scalars = total[0:16], total[16:17]
    s, t, rr = column(scalars, 0), column(scalars, 16), column(scalars, 32)
    own_r = own_ref[:, 0:64]
    bb, bw = own_ref[:, 64:65], own_ref[:, 65:66]
    alpha0 = bb / bw
    beta = rr / bb
    alpha1 = rr / (s + 2.0 * beta * t + beta * beta * bw)
    target = side_ref[:, 0:64]
    solution_ref[...] = alpha0 * target + alpha1 * (own_r + beta * target)
    post_ref[...] = (alpha0 + alpha1 * beta) * mean[:, :64] + alpha1 * mean[:, 64:]


def shape(*dims, dtype=F32):
    return jax.ShapeDtypeStruct(dims, dtype)


def in_hbm(array):
    return pltpu.with_memory_space_constraint(array, pltpu.HBM)


def per_device(train_points, cand_points, inv_length, noise, targets):
    def call(kernel, **options):
        return pl.pallas_call(kernel, compiler_params=PARAMS, **options)

    vmem = pl.BlockSpec(memory_space=pltpu.VMEM)
    hbm = pl.BlockSpec(memory_space=pltpu.HBM)
    build = [
        pltpu.VMEM((128, ROWS), BF16),
        pltpu.VMEM((128, ROWS), F32),
        pltpu.VMEM((128, ROWS), F32),
    ]
    build_cost = pl.CostEstimate(
        flops=2 * ROWS * COLS * 160, bytes_accessed=2 * ROWS * COLS, transcendentals=2 * ROWS * COLS
    )

    y_out, z_out, side = call(
        prepare,
        in_specs=[hbm] * 5,
        out_shape=(
            shape(NQ, 80, 128, dtype=BF16),
            shape(NZ, 48, 128, dtype=BF16),
            shape(RHS, 128),
        ),
        scratch_shapes=[
            pltpu.VMEM((D, S), F32),
            pltpu.VMEM((D, S), F32),
            pltpu.VMEM((1, D), F32),
            pltpu.VMEM((1, S), F32),
            pltpu.VMEM((RHS, S), F32),
            pltpu.SemaphoreType.DMA((5,)),
        ],
    )(
        in_hbm(train_points),
        in_hbm(cand_points),
        in_hbm(inv_length.reshape(1, D)),
        in_hbm(noise.reshape(1, S)),
        in_hbm(targets),
    )
    z_in = lax.all_gather(lax.all_to_all(z_out, "z", 0, 0), "c", axis=0)
    y_in = lax.all_to_all(y_out, ("y", "x"), 0, 0)
    col, b_col = call(
        col_side,
        out_shape=(shape(COLS, 128, dtype=BF16), shape(32, COLS, dtype=BF16)),
        cost_estimate=pl.CostEstimate(
            flops=COLS * 1000, bytes_accessed=4 * COLS * 128, transcendentals=0
        ),
    )(z_in)
    kern, kept, image_out = call(
        first_apply,
        out_specs=(hbm, vmem, vmem),
        out_shape=(
            pltpu.HBM((STORED * PIECE, ROWS), BF16),
            shape(KEPT * PIECE, ROWS, dtype=BF16),
            shape(NQ, RHS, ROWS, dtype=BF16),
        ),
        scratch_shapes=[
            pltpu.VMEM((RHS, ROWS), F32),
            *build,
            pltpu.VMEM((COLS, ROWS), BF16),
            pltpu.SemaphoreType.DMA((STORED,)),
        ],
        cost_estimate=build_cost,
    )(y_in, col, b_col, side)
    image_in = lax.all_to_all(image_out, ("y", "x"), 0, 0)
    w_out, w_row, b_row = call(
        merge_image,
        out_shape=(shape(NZ, RHS, 128, dtype=BF16), shape(RHS, ROWS), shape(RHS, ROWS)),
    )(image_in, y_in)
    w_in = lax.all_gather(lax.all_to_all(w_out, "z", 0, 0), "c", axis=0)
    scalar_out, r_col, own = call(
        second_apply,
        in_specs=[vmem] * 4 + [hbm, vmem, vmem],
        out_shape=(shape(NZ, 1, 128), shape(32, COLS, dtype=BF16), shape(RHS, 128)),
        scratch_shapes=[
            pltpu.VMEM((STORED * PIECE, ROWS), BF16),
            pltpu.SemaphoreType.DMA((READS,)),
        ],
    )(w_in, b_col, w_row, b_row, in_hbm(kern), kept, side)
    scalar_in = lax.all_gather(lax.all_to_all(scalar_out, "z", 0, 0), "c", axis=0)
    mean_part = call(
        cand_mean,
        out_shape=shape(NQ, RHS, 128),
        scratch_shapes=[*build, *[pltpu.VMEM((COLS, ROWS), BF16)] * 2],
        cost_estimate=build_cost,
    )(y_in, col, b_col, r_col)
    mean_out = call(pack, out_shape=shape(NQ, 24, 128))(scalar_in, mean_part)
    mean_in = lax.all_to_all(mean_out, ("y", "x"), 0, 0)
    return call(finish, out_shape=(shape(RHS, S), shape(RHS, S)))(mean_in, own, side)


def solution(mesh):
    fine = Mesh(mesh.devices.reshape(16, 2, 4, 4), ("z", "c", "y", "x"))
    every = ("z", "c", "y", "x")
    wide = P(None, every)
    return jax.shard_map(
        per_device,
        mesh=fine,
        in_specs=(wide, wide, P(), P(every), wide),
        out_specs=(wide, wide),
        check_vma=False,
    )
```

```python
import math

import jax
import jax.numpy as jnp
from jax import lax
from jax.experimental import pallas as pl
from jax.experimental.pallas import tpu as pltpu
from jax.sharding import Mesh, PartitionSpec as P

F32 = jnp.float32
BF16 = jnp.bfloat16

D = 64
S = 64
RHS = 16
NQ = 16
NZ = 16
ROWS = NQ * S
COLS = 2 * NZ * S
LOG2E = math.log2(math.e)
CHUNKS = 4
PIECE = COLS // CHUNKS
KEPT = 1
STORED = CHUNKS - KEPT
READ = 256
READS = STORED * PIECE // READ
PARAMS = pltpu.CompilerParams(vmem_limit_bytes=24 * 1024 * 1024)


def halves(value):
    high = value.astype(BF16)
    return high, (value - high.astype(F32)).astype(BF16)


def thirds(value):
    high = value.astype(BF16).astype(F32)
    rest = value - high
    middle = rest.astype(BF16).astype(F32)
    low = (rest - middle).astype(BF16).astype(F32)
    return high, middle, low


def rows_of(width, pieces):
    index = lax.broadcasted_iota(jnp.int32, (16, width), 0)
    total = jnp.zeros((16, width), F32)
    for i, piece in enumerate(pieces):
        total = jnp.where(index == i, piece, total)
    return total


def column(row, start):
    lane = lax.broadcasted_iota(jnp.int32, (RHS, 128), 1)
    index = lax.broadcasted_iota(jnp.int32, (RHS, 128), 0)
    return jnp.sum(jnp.where(lane == index + start, row, 0.0), axis=1, keepdims=True)


def prepare(
    train_hbm, cand_hbm, inv_hbm, noise_hbm, target_hbm, y_ref, z_ref, side_ref,
    train_ref, cand_ref, inv_ref, noise_ref, target_ref, sems,
):
    copies = [
        pltpu.make_async_copy(source, target, sems.at[i])
        for i, (source, target) in enumerate(
            [
                (train_hbm, train_ref),
                (inv_hbm, inv_ref),
                (target_hbm, target_ref),
                (cand_hbm, cand_ref),
                (noise_hbm, noise_ref),
            ]
        )
    ]
    for copy in copies:
        copy.start()
    for copy in copies:
        copy.wait()
    eye = lax.broadcasted_iota(jnp.int32, (D, D), 0) == lax.broadcasted_iota(
        jnp.int32, (D, D), 1
    )
    inv = jnp.sum(jnp.where(eye, inv_ref[...], 0.0), axis=1, keepdims=True)
    train = train_ref[...] * inv
    cand = cand_ref[...] * inv
    target = target_ref[...]
    b_high, b_low = halves(target)
    b = jnp.concatenate([b_high, b_low], axis=1)
    both = jnp.concatenate([train.astype(BF16), cand.astype(BF16)], axis=1)
    folded = jnp.concatenate([train[:32].astype(BF16), train[32:].astype(BF16)], axis=1)
    for i in range(NZ):
        z_ref[i, 0:32, :] = folded
        z_ref[i, 32:48, :] = b
    y_ref[0:64, :] = both
    y_ref[64:80, :] = b
    side_ref[...] = jnp.concatenate(
        [target, jnp.broadcast_to(noise_ref[...], (RHS, S))], axis=1
    )


def order(own_ref, one_ref, two_ref, three_ref, out_ref):
    y = lax.axis_index("y")
    for k, ref in enumerate([own_ref, one_ref, two_ref, three_ref]):
        value = ref[...]
        for x in range(4):
            out_ref[x, (y + k) % 4] = value


def row_side(y_ref, j, first):
    points = jnp.concatenate(
        [y_ref[(2 * j) % 4, j // 2, 0:64, first : first + 64],
            y_ref[(2 * j + 1) % 4, j // 2, 0:64, first : first + 64],
       ],
        axis=1,
    ).astype(F32)
    norm = jnp.sum(points * points, axis=0, keepdims=True)
    extra = rows_of(128, [*thirds(norm), 1.0, 1.0, 1.0])
    return jnp.concatenate(
        [-2.0 * points, extra, jnp.zeros((48, 128), F32)], axis=0
    ).astype(BF16)


def col_side(z_ref, col_ref, b_ref):
    for z in range(NZ):
        low, high = z_ref[0, z].astype(F32), z_ref[1, z].astype(F32)
        first = jnp.concatenate([low[:, :64], high[:, :64]], axis=1)
        second = jnp.concatenate([low[:, 64:], high[:, 64:]], axis=1)
        points = jnp.concatenate([first[0:32], second[0:32]], axis=0)
        b_ref[:, z * 128 : z * 128 + 128] = jnp.concatenate(
            [first[32:48], second[32:48]], axis=0
        ).astype(BF16)
        norm = jnp.sum(points * points, axis=0, keepdims=True)
        extra = rows_of(128, [1.0, 1.0, 1.0, *thirds(norm)])
        full = jnp.concatenate([points, extra, jnp.zeros((48, 128), F32)], axis=0)
        col_ref[z * 128 : z * 128 + 128, :] = full.T.astype(BF16)


def matern_of(inner):
    five_dist = jnp.maximum(inner, 1e-30) * 5.0
    scaled = five_dist * lax.rsqrt(five_dist)
    return (1.0 + scaled + five_dist * (1.0 / 3.0)) * jnp.exp2(scaled * (-LOG2E))


def piece(tile_ref, hbm_ref, sems, i):
    span = pl.ds(pl.multiple_of(i * PIECE, PIECE), PIECE)
    return tile_ref.at[span, :], hbm_ref.at[span, :], sems.at[i]


def fill(col_ref, row_ref, kern_ref, even_ref, odd_ref, before=None, low_ref=None):
    def inner(z, out_ref):
        points = col_ref[pl.ds(pl.multiple_of(z * 128, 128), 128), :]
        out_ref[...] = jnp.dot(points, row_ref[...], preferred_element_type=F32)

    def spread(z, in_ref):
        for i in range(8):
            span = pl.ds(pl.multiple_of(z * 128 + i * 16, 16), 16)
            kern = matern_of(in_ref[i * 16 : i * 16 + 16, :])
            if low_ref is None:
                kern_ref[span, :] = kern.astype(BF16)
            else:
                high, low = halves(kern)
                kern_ref[span, :] = high
                low_ref[span, :] = low

    def step(i, _):
        if before is not None:
            before(i)
        buffers = [even_ref, odd_ref]
        for k in range(4):
            z = 4 * i + k
            inner(jnp.minimum(z + 1, NZ - 1), buffers[(k + 1) % 2])
            spread(z, buffers[k % 2])
        return 0

    inner(0, even_ref)
    lax.fori_loop(0, NZ // 4, step, 0)


def own_block(q):
    return pl.ds(pl.multiple_of((q // 2) * 128, 128), 128)


def own_mask(q):
    lane = lax.broadcasted_iota(jnp.int32, (RHS, 128), 1)
    return (lane // 64) == (q % 2)


def position():
    return lax.axis_index("y") * 4 + lax.axis_index("x")


def first_apply(
    y_ref, col_ref, b_ref, side_ref, hbm_ref, kept_ref, out_ref,
    acc_ref, row_ref, even_ref, odd_ref, kern_ref, sems,
):
    q = position()
    for j in range(NQ // 2):
        row_ref[:, j * 128 : j * 128 + 128] = row_side(y_ref, j, 0)

    def before(i):
        @pl.when(i > 0)
        def _():
            pltpu.make_async_copy(*piece(kern_ref, hbm_ref, sems, i - 1)).start()

    fill(col_ref, row_ref, kern_ref, even_ref, odd_ref, before)
    total = jnp.dot(b_ref[...], kern_ref[...], preferred_element_type=F32)
    acc_ref[...] = total[0:16] + total[16:32]
    kept_ref[...] = kern_ref[STORED * PIECE :, :]
    own = side_ref[:, 0:64] * side_ref[:, 64:128]
    twice = jnp.concatenate([own, own], axis=1)
    acc_ref[:, own_block(q)] += jnp.where(own_mask(q), twice, 0.0)
    image = acc_ref[...].astype(BF16)
    for i in range(NQ):
        out_ref[i] = image
    for i in range(STORED):
        pltpu.make_async_copy(*piece(kern_ref, hbm_ref, sems, i)).wait()


def merge_image(part_ref, y_ref, out_ref, w_ref, br_ref):
    q = position()
    total = part_ref[0].astype(F32)
    for i in range(1, NQ):
        total = total + part_ref[i].astype(F32)
    w_ref[...] = total
    for j in range(NQ // 2):
        even = y_ref[(2 * j) % 4, j // 2, 64:80, :].astype(F32)
        odd = y_ref[(2 * j + 1) % 4, j // 2, 64:80, :].astype(F32)
        br_ref[:, j * 128 : j * 128 + 128] = jnp.concatenate(
            [even[:, :64] + even[:, 64:], odd[:, :64] + odd[:, 64:]], axis=1
        )
    b = br_ref[...]
    bw = jnp.sum(b * total, axis=1, keepdims=True)
    bb = jnp.sum(b * b, axis=1, keepdims=True)
    block = w_ref[:, own_block(q)]
    own = jnp.where(q % 2 == 0, block[:, :64], block[:, 64:])
    lane = lax.broadcasted_iota(jnp.int32, (RHS, 64), 1)
    scalars = jnp.zeros((RHS, 64), F32)
    for i, piece in enumerate([*thirds(bw), *thirds(bb)]):
        scalars = jnp.where(lane == i, piece, scalars)
    message = jnp.concatenate([own, scalars], axis=1).astype(BF16)
    for i in range(NZ):
        out_ref[i] = message


def fetch(hbm_ref, tile_ref, sems, i):
    span = slice(i * READ, i * READ + READ)
    return pltpu.make_async_copy(hbm_ref.at[span, :], tile_ref.at[span, :], sems.at[i])


def streamed(r_ref, hbm_ref, tile_ref, sems, kept_ref):
    total = jnp.dot(r_ref[:, STORED * PIECE :], kept_ref[...], preferred_element_type=F32)
    for i in range(READS):
        fetch(hbm_ref, tile_ref, sems, i).wait()
        span = slice(i * READ, i * READ + READ)
        total = total + jnp.dot(r_ref[:, span], tile_ref[span, :], preferred_element_type=F32)
    return total[0:16] + total[16:32]


def second_apply(
    s_ref, b_ref, w_ref, br_ref, kern_hbm, kept_ref, side_ref, out_ref, r_ref, own_ref,
    kern_ref, sems,
):
    for i in range(READS):
        fetch(kern_hbm, kern_ref, sems, i).start()
    q = position()
    sums = s_ref[0, 0, :, 64:128].astype(F32)
    for c in range(2):
        for z in range(NZ):
            if c or z:
                sums = sums + s_ref[c, z, :, 64:128].astype(F32)
    lane = lax.broadcasted_iota(jnp.int32, (RHS, 64), 1)
    bw = jnp.sum(jnp.where(lane < 3, sums, 0.0), axis=1, keepdims=True)
    bb = jnp.sum(jnp.where((lane >= 3) & (lane < 6), sums, 0.0), axis=1, keepdims=True)
    alpha = bb / bw
    for z in range(NZ):
        span = slice(z * 128, z * 128 + 128)
        w = jnp.concatenate([s_ref[0, z, :, 0:64], s_ref[1, z, :, 0:64]], axis=1).astype(F32)
        b = b_ref[0:16, span].astype(F32) + b_ref[16:32, span].astype(F32)
        high, low = halves(b - alpha * w)
        r_ref[:, span] = jnp.concatenate([high, low], axis=0)
    r_row = br_ref[...] - alpha * w_ref[...]
    block = w_ref[:, own_block(q)]
    own_w = jnp.where(q % 2 == 0, block[:, :64], block[:, 64:])
    target, noise = side_ref[:, 0:64], side_ref[:, 64:128]
    own_r = target - alpha * own_w
    t = jnp.sum(own_r * own_w, axis=1, keepdims=True)
    rr = jnp.sum(own_r * own_r, axis=1, keepdims=True)
    side = jnp.where(lane == 0, bb, jnp.where(lane == 1, bw, 0.0))
    own_ref[...] = jnp.concatenate([own_r, side], axis=1)
    applied = streamed(r_ref, kern_hbm, kern_ref, sems, kept_ref)
    s = jnp.sum(r_row * applied, axis=1, keepdims=True) + jnp.sum(
        noise * own_r * own_r, axis=1, keepdims=True
    )
    wide = lax.broadcasted_iota(jnp.int32, (RHS, 128), 1)
    index = lax.broadcasted_iota(jnp.int32, (RHS, 128), 0)
    spread = (
        jnp.where(wide == index, s, 0.0)
        + jnp.where(wide == index + 16, t, 0.0)
        + jnp.where(wide == index + 32, rr, 0.0)
    )
    spread = jnp.sum(spread, axis=0, keepdims=True)
    for i in range(NZ):
        out_ref[i] = spread


def cand_mean(
    y_ref, col_ref, b_ref, r_ref, out_ref, row_ref, even_ref, odd_ref, kern_ref, low_ref
):
    for j in range(NQ // 2):
        row_ref[:, j * 128 : j * 128 + 128] = row_side(y_ref, j, 64)
    fill(col_ref, row_ref, kern_ref, even_ref, odd_ref, low_ref=low_ref)
    vectors = jnp.concatenate([b_ref[...], r_ref[...]], axis=0)
    total = jnp.dot(vectors, kern_ref[...], preferred_element_type=F32) + jnp.dot(
        vectors, low_ref[...], preferred_element_type=F32
    )
    mean0, mean = total[0:16] + total[16:32], total[32:48] + total[48:64]
    for i in range(NQ):
        span = slice(i * 64, i * 64 + 64)
        out_ref[i] = jnp.concatenate([mean0[:, span], mean[:, span]], axis=1)


def pack(s_ref, mean_ref, out_ref):
    total = s_ref[0, 0]
    for c in range(2):
        for z in range(NZ):
            if c or z:
                total = total + s_ref[c, z]
    eight = lax.broadcasted_iota(jnp.int32, (8, 128), 0)
    total = jnp.where(eight == 0, total, 0.0)
    for i in range(NQ):
        out_ref[i, 0:16, :] = mean_ref[i]
        out_ref[i, 16:24, :] = total


def finish(part_ref, own_ref, side_ref, solution_ref, post_ref):
    total = part_ref[0]
    for i in range(1, NQ):
        total = total + part_ref[i]
    mean, scalars = total[0:16], total[16:17]
    s, t, rr = column(scalars, 0), column(scalars, 16), column(scalars, 32)
    own_r = own_ref[:, 0:64]
    bb, bw = own_ref[:, 64:65], own_ref[:, 65:66]
    alpha0 = bb / bw
    beta = rr / bb
    alpha1 = rr / (s + 2.0 * beta * t + beta * beta * bw)
    target = side_ref[:, 0:64]
    solution_ref[...] = alpha0 * target + alpha1 * (own_r + beta * target)
    post_ref[...] = (alpha0 + alpha1 * beta) * mean[:, :64] + alpha1 * mean[:, 64:]


def shape(*dims, dtype=F32):
    return jax.ShapeDtypeStruct(dims, dtype)


def in_hbm(array):
    return pltpu.with_memory_space_constraint(array, pltpu.HBM)


def per_device(train_points, cand_points, inv_length, noise, targets):
    def call(kernel, **options):
        return pl.pallas_call(kernel, compiler_params=PARAMS, **options)

    vmem = pl.BlockSpec(memory_space=pltpu.VMEM)
    hbm = pl.BlockSpec(memory_space=pltpu.HBM)
    build = [
        pltpu.VMEM((128, ROWS), BF16),
        pltpu.VMEM((128, ROWS), F32),
        pltpu.VMEM((128, ROWS), F32),
    ]
    build_cost = pl.CostEstimate(
        flops=2 * ROWS * COLS * 160, bytes_accessed=2 * ROWS * COLS, transcendentals=2 * ROWS * COLS
    )

    y_out, z_out, side = call(
        prepare,
        in_specs=[hbm] * 5,
        out_shape=(
            shape(80, 128, dtype=BF16),
            shape(NZ, 48, 128, dtype=BF16),
            shape(RHS, 128),
        ),
        scratch_shapes=[
            pltpu.VMEM((D, S), F32),
            pltpu.VMEM((D, S), F32),
            pltpu.VMEM((1, D), F32),
            pltpu.VMEM((1, S), F32),
            pltpu.VMEM((RHS, S), F32),
            pltpu.SemaphoreType.DMA((5,)),
        ],
    )(
        in_hbm(train_points),
        in_hbm(cand_points),
        in_hbm(inv_length.reshape(1, D)),
        in_hbm(noise.reshape(1, S)),
        in_hbm(targets),
    )
    z_in = lax.all_gather(lax.all_to_all(z_out, "z", 0, 0), "c", axis=0)
    along_y = [
        lax.ppermute(y_out, "y", [((d + k) % 4, d) for d in range(4)]) for k in (1, 2, 3)
    ]
    y_half = call(
        order,
        out_shape=shape(4, 4, 80, 128, dtype=BF16),
        cost_estimate=pl.CostEstimate(flops=0, bytes_accessed=400000, transcendentals=0),
    )(y_out, *along_y)
    y_in = lax.all_to_all(y_half, "x", 0, 0)
    col, b_col = call(
        col_side,
        out_shape=(shape(COLS, 128, dtype=BF16), shape(32, COLS, dtype=BF16)),
        cost_estimate=pl.CostEstimate(
            flops=COLS * 1000, bytes_accessed=4 * COLS * 128, transcendentals=0
        ),
    )(z_in)
    kern, kept, image_out = call(
        first_apply,
        out_specs=(hbm, vmem, vmem),
        out_shape=(
            pltpu.HBM((STORED * PIECE, ROWS), BF16),
            shape(KEPT * PIECE, ROWS, dtype=BF16),
            shape(NQ, RHS, ROWS, dtype=BF16),
        ),
        scratch_shapes=[
            pltpu.VMEM((RHS, ROWS), F32),
            *build,
            pltpu.VMEM((COLS, ROWS), BF16),
            pltpu.SemaphoreType.DMA((STORED,)),
        ],
        cost_estimate=build_cost,
    )(y_in, col, b_col, side)
    image_in = lax.all_to_all(image_out, ("y", "x"), 0, 0)
    w_out, w_row, b_row = call(
        merge_image,
        out_shape=(shape(NZ, RHS, 128, dtype=BF16), shape(RHS, ROWS), shape(RHS, ROWS)),
    )(image_in, y_in)
    w_in = lax.all_gather(lax.all_to_all(w_out, "z", 0, 0), "c", axis=0)
    scalar_out, r_col, own = call(
        second_apply,
        in_specs=[vmem] * 4 + [hbm, vmem, vmem],
        out_shape=(shape(NZ, 1, 128), shape(32, COLS, dtype=BF16), shape(RHS, 128)),
        scratch_shapes=[
            pltpu.VMEM((STORED * PIECE, ROWS), BF16),
            pltpu.SemaphoreType.DMA((READS,)),
        ],
    )(w_in, b_col, w_row, b_row, in_hbm(kern), kept, side)
    scalar_in = lax.all_gather(lax.all_to_all(scalar_out, "z", 0, 0), "c", axis=0)
    mean_part = call(
        cand_mean,
        out_shape=shape(NQ, RHS, 128),
        scratch_shapes=[*build, *[pltpu.VMEM((COLS, ROWS), BF16)] * 2],
        cost_estimate=build_cost,
    )(y_in, col, b_col, r_col)
    mean_out = call(pack, out_shape=shape(NQ, 24, 128))(scalar_in, mean_part)
    mean_in = lax.all_to_all(mean_out, ("y", "x"), 0, 0)
    return call(finish, out_shape=(shape(RHS, S), shape(RHS, S)))(mean_in, own, side)


def solution(mesh):
    fine = Mesh(mesh.devices.reshape(16, 2, 4, 4), ("z", "c", "y", "x"))
    every = ("z", "c", "y", "x")
    wide = P(None, every)
    return jax.shard_map(
        per_device,
        mesh=fine,
        in_specs=(wide, wide, P(), P(every), wide),
        out_specs=(wide, wide),
        check_vma=False,
    )
```

```python
import math

import jax
import jax.numpy as jnp
from jax import lax
from jax.experimental import pallas as pl
from jax.experimental.pallas import tpu as pltpu
from jax.sharding import Mesh, PartitionSpec as P

F32 = jnp.float32
BF16 = jnp.bfloat16

D = 64
S = 64
RHS = 16
NQ = 16
NZ = 16
ROWS = NQ * S
COLS = 2 * NZ * S
LOG2E = math.log2(math.e)
CHUNKS = 4
PIECE = COLS // CHUNKS
KEPT = 1
STORED = CHUNKS - KEPT
READ = 256
READS = STORED * PIECE // READ
PARAMS = pltpu.CompilerParams(vmem_limit_bytes=24 * 1024 * 1024)


def halves(value):
    high = value.astype(BF16)
    return high, (value - high.astype(F32)).astype(BF16)


def thirds(value):
    high = value.astype(BF16).astype(F32)
    rest = value - high
    middle = rest.astype(BF16).astype(F32)
    low = (rest - middle).astype(BF16).astype(F32)
    return high, middle, low


def rows_of(width, pieces):
    index = lax.broadcasted_iota(jnp.int32, (16, width), 0)
    total = jnp.zeros((16, width), F32)
    for i, piece in enumerate(pieces):
        total = jnp.where(index == i, piece, total)
    return total


def column(row, start):
    lane = lax.broadcasted_iota(jnp.int32, (RHS, 128), 1)
    index = lax.broadcasted_iota(jnp.int32, (RHS, 128), 0)
    return jnp.sum(jnp.where(lane == index + start, row, 0.0), axis=1, keepdims=True)


def prepare(
    train_hbm, cand_hbm, inv_hbm, noise_hbm, target_hbm, y_ref, z_ref, side_ref,
    train_ref, cand_ref, inv_ref, noise_ref, target_ref, sems,
):
    copies = [
        pltpu.make_async_copy(source, target, sems.at[i])
        for i, (source, target) in enumerate(
            [
                (train_hbm, train_ref),
                (inv_hbm, inv_ref),
                (target_hbm, target_ref),
                (cand_hbm, cand_ref),
                (noise_hbm, noise_ref),
            ]
        )
    ]
    for copy in copies:
        copy.start()
    for copy in copies:
        copy.wait()
    eye = lax.broadcasted_iota(jnp.int32, (D, D), 0) == lax.broadcasted_iota(
        jnp.int32, (D, D), 1
    )
    inv = jnp.sum(jnp.where(eye, inv_ref[...], 0.0), axis=1, keepdims=True)
    train = train_ref[...] * inv
    cand = cand_ref[...] * inv
    target = target_ref[...]
    b_high, b_low = halves(target)
    b = jnp.concatenate([b_high, b_low], axis=1)
    both = jnp.concatenate([train.astype(BF16), cand.astype(BF16)], axis=1)
    folded = jnp.concatenate([train[:32].astype(BF16), train[32:].astype(BF16)], axis=1)
    for i in range(NZ):
        z_ref[i, 0:32, :] = folded
        z_ref[i, 32:48, :] = b
    y_ref[0:64, :] = both
    y_ref[64:80, :] = b
    side_ref[...] = jnp.concatenate(
        [target, jnp.broadcast_to(noise_ref[...], (RHS, S))], axis=1
    )


def order(own_ref, far_ref, out_ref):
    far = lax.axis_index("far")
    for k, ref in enumerate([own_ref, far_ref]):
        value = ref[...]
        for i in range(8):
            out_ref[i, (far + k) % 2] = value


def shard(ref, q, rows, lanes=slice(None)):
    y, x = q // 4, q % 4
    return ref[(y % 2) * 4 + x, y // 2, rows, lanes]


def row_side(y_ref, j, first):
    points = jnp.concatenate(
        [
            shard(y_ref, 2 * j, slice(0, 64), slice(first, first + 64)),
            shard(y_ref, 2 * j + 1, slice(0, 64), slice(first, first + 64)),
        ],
        axis=1,
    ).astype(F32)
    norm = jnp.sum(points * points, axis=0, keepdims=True)
    extra = rows_of(128, [*thirds(norm), 1.0, 1.0, 1.0])
    return jnp.concatenate(
        [-2.0 * points, extra, jnp.zeros((48, 128), F32)], axis=0
    ).astype(BF16)


def col_side(z_ref, col_ref, b_ref):
    for z in range(NZ):
        low, high = z_ref[0, z].astype(F32), z_ref[1, z].astype(F32)
        first = jnp.concatenate([low[:, :64], high[:, :64]], axis=1)
        second = jnp.concatenate([low[:, 64:], high[:, 64:]], axis=1)
        points = jnp.concatenate([first[0:32], second[0:32]], axis=0)
        b_ref[:, z * 128 : z * 128 + 128] = jnp.concatenate(
            [first[32:48], second[32:48]], axis=0
        ).astype(BF16)
        norm = jnp.sum(points * points, axis=0, keepdims=True)
        extra = rows_of(128, [1.0, 1.0, 1.0, *thirds(norm)])
        full = jnp.concatenate([points, extra, jnp.zeros((48, 128), F32)], axis=0)
        col_ref[z * 128 : z * 128 + 128, :] = full.T.astype(BF16)


def matern_of(inner):
    five_dist = jnp.maximum(inner, 1e-30) * 5.0
    scaled = five_dist * lax.rsqrt(five_dist)
    return (1.0 + scaled + five_dist * (1.0 / 3.0)) * jnp.exp2(scaled * (-LOG2E))


def piece(tile_ref, hbm_ref, sems, i):
    span = pl.ds(pl.multiple_of(i * PIECE, PIECE), PIECE)
    return tile_ref.at[span, :], hbm_ref.at[span, :], sems.at[i]


def fill(col_ref, row_ref, kern_ref, even_ref, odd_ref, before=None, low_ref=None):
    def inner(z, out_ref):
        points = col_ref[pl.ds(pl.multiple_of(z * 128, 128), 128), :]
        out_ref[...] = jnp.dot(points, row_ref[...], preferred_element_type=F32)

    def spread(z, in_ref):
        for i in range(8):
            span = pl.ds(pl.multiple_of(z * 128 + i * 16, 16), 16)
            kern = matern_of(in_ref[i * 16 : i * 16 + 16, :])
            if low_ref is None:
                kern_ref[span, :] = kern.astype(BF16)
            else:
                high, low = halves(kern)
                kern_ref[span, :] = high
                low_ref[span, :] = low

    def step(i, _):
        if before is not None:
            before(i)
        buffers = [even_ref, odd_ref]
        for k in range(4):
            z = 4 * i + k
            inner(jnp.minimum(z + 1, NZ - 1), buffers[(k + 1) % 2])
            spread(z, buffers[k % 2])
        return 0

    inner(0, even_ref)
    lax.fori_loop(0, NZ // 4, step, 0)


def own_block(q):
    return pl.ds(pl.multiple_of((q // 2) * 128, 128), 128)


def own_mask(q):
    lane = lax.broadcasted_iota(jnp.int32, (RHS, 128), 1)
    return (lane // 64) == (q % 2)


def position():
    return (lax.axis_index("far") * 2 + lax.axis_index("near")) * 4 + lax.axis_index("x")


def first_apply(
    y_ref, col_ref, b_ref, side_ref, hbm_ref, kept_ref, out_ref,
    acc_ref, row_ref, even_ref, odd_ref, kern_ref, sems,
):
    q = position()
    for j in range(NQ // 2):
        row_ref[:, j * 128 : j * 128 + 128] = row_side(y_ref, j, 0)

    def before(i):
        @pl.when(i > 0)
        def _():
            pltpu.make_async_copy(*piece(kern_ref, hbm_ref, sems, i - 1)).start()

    fill(col_ref, row_ref, kern_ref, even_ref, odd_ref, before)
    total = jnp.dot(b_ref[...], kern_ref[...], preferred_element_type=F32)
    acc_ref[...] = total[0:16] + total[16:32]
    kept_ref[...] = kern_ref[STORED * PIECE :, :]
    own = side_ref[:, 0:64] * side_ref[:, 64:128]
    twice = jnp.concatenate([own, own], axis=1)
    acc_ref[:, own_block(q)] += jnp.where(own_mask(q), twice, 0.0)
    image = acc_ref[...].astype(BF16)
    for i in range(NQ):
        out_ref[i] = image
    for i in range(STORED):
        pltpu.make_async_copy(*piece(kern_ref, hbm_ref, sems, i)).wait()


def merge_image(part_ref, y_ref, out_ref, w_ref, br_ref):
    q = position()
    total = part_ref[0].astype(F32)
    for i in range(1, NQ):
        total = total + part_ref[i].astype(F32)
    w_ref[...] = total
    for j in range(NQ // 2):
        even = shard(y_ref, 2 * j, slice(64, 80)).astype(F32)
        odd = shard(y_ref, 2 * j + 1, slice(64, 80)).astype(F32)
        br_ref[:, j * 128 : j * 128 + 128] = jnp.concatenate(
            [even[:, :64] + even[:, 64:], odd[:, :64] + odd[:, 64:]], axis=1
        )
    b = br_ref[...]
    bw = jnp.sum(b * total, axis=1, keepdims=True)
    bb = jnp.sum(b * b, axis=1, keepdims=True)
    block = w_ref[:, own_block(q)]
    own = jnp.where(q % 2 == 0, block[:, :64], block[:, 64:])
    lane = lax.broadcasted_iota(jnp.int32, (RHS, 64), 1)
    scalars = jnp.zeros((RHS, 64), F32)
    for i, piece in enumerate([*thirds(bw), *thirds(bb)]):
        scalars = jnp.where(lane == i, piece, scalars)
    message = jnp.concatenate([own, scalars], axis=1).astype(BF16)
    for i in range(NZ):
        out_ref[i] = message


def fetch(hbm_ref, tile_ref, sems, i):
    span = slice(i * READ, i * READ + READ)
    return pltpu.make_async_copy(hbm_ref.at[span, :], tile_ref.at[span, :], sems.at[i])


def streamed(r_ref, hbm_ref, tile_ref, sems, kept_ref):
    total = jnp.dot(r_ref[:, STORED * PIECE :], kept_ref[...], preferred_element_type=F32)
    for i in range(READS):
        fetch(hbm_ref, tile_ref, sems, i).wait()
        span = slice(i * READ, i * READ + READ)
        total = total + jnp.dot(r_ref[:, span], tile_ref[span, :], preferred_element_type=F32)
    return total[0:16] + total[16:32]


def second_apply(
    s_ref, b_ref, w_ref, br_ref, kern_hbm, kept_ref, side_ref, out_ref, r_ref, own_ref,
    kern_ref, sems,
):
    for i in range(READS):
        fetch(kern_hbm, kern_ref, sems, i).start()
    q = position()
    sums = s_ref[0, 0, :, 64:128].astype(F32)
    for c in range(2):
        for z in range(NZ):
            if c or z:
                sums = sums + s_ref[c, z, :, 64:128].astype(F32)
    lane = lax.broadcasted_iota(jnp.int32, (RHS, 64), 1)
    bw = jnp.sum(jnp.where(lane < 3, sums, 0.0), axis=1, keepdims=True)
    bb = jnp.sum(jnp.where((lane >= 3) & (lane < 6), sums, 0.0), axis=1, keepdims=True)
    alpha = bb / bw
    for z in range(NZ):
        span = slice(z * 128, z * 128 + 128)
        w = jnp.concatenate([s_ref[0, z, :, 0:64], s_ref[1, z, :, 0:64]], axis=1).astype(F32)
        b = b_ref[0:16, span].astype(F32) + b_ref[16:32, span].astype(F32)
        high, low = halves(b - alpha * w)
        r_ref[:, span] = jnp.concatenate([high, low], axis=0)
    r_row = br_ref[...] - alpha * w_ref[...]
    block = w_ref[:, own_block(q)]
    own_w = jnp.where(q % 2 == 0, block[:, :64], block[:, 64:])
    target, noise = side_ref[:, 0:64], side_ref[:, 64:128]
    own_r = target - alpha * own_w
    t = jnp.sum(own_r * own_w, axis=1, keepdims=True)
    rr = jnp.sum(own_r * own_r, axis=1, keepdims=True)
    side = jnp.where(lane == 0, bb, jnp.where(lane == 1, bw, 0.0))
    own_ref[...] = jnp.concatenate([own_r, side], axis=1)
    applied = streamed(r_ref, kern_hbm, kern_ref, sems, kept_ref)
    s = jnp.sum(r_row * applied, axis=1, keepdims=True) + jnp.sum(
        noise * own_r * own_r, axis=1, keepdims=True
    )
    wide = lax.broadcasted_iota(jnp.int32, (RHS, 128), 1)
    index = lax.broadcasted_iota(jnp.int32, (RHS, 128), 0)
    spread = (
        jnp.where(wide == index, s, 0.0)
        + jnp.where(wide == index + 16, t, 0.0)
        + jnp.where(wide == index + 32, rr, 0.0)
    )
    spread = jnp.sum(spread, axis=0, keepdims=True)
    for i in range(NZ):
        out_ref[i] = spread


def cand_mean(
    y_ref, col_ref, b_ref, r_ref, out_ref, row_ref, even_ref, odd_ref, kern_ref, low_ref
):
    for j in range(NQ // 2):
        row_ref[:, j * 128 : j * 128 + 128] = row_side(y_ref, j, 64)
    fill(col_ref, row_ref, kern_ref, even_ref, odd_ref, low_ref=low_ref)
    vectors = jnp.concatenate([b_ref[...], r_ref[...]], axis=0)
    total = jnp.dot(vectors, kern_ref[...], preferred_element_type=F32) + jnp.dot(
        vectors, low_ref[...], preferred_element_type=F32
    )
    mean0, mean = total[0:16] + total[16:32], total[32:48] + total[48:64]
    for i in range(NQ):
        span = slice(i * 64, i * 64 + 64)
        out_ref[i] = jnp.concatenate([mean0[:, span], mean[:, span]], axis=1)


def pack(s_ref, mean_ref, out_ref):
    total = s_ref[0, 0]
    for c in range(2):
        for z in range(NZ):
            if c or z:
                total = total + s_ref[c, z]
    eight = lax.broadcasted_iota(jnp.int32, (8, 128), 0)
    total = jnp.where(eight == 0, total, 0.0)
    for i in range(NQ):
        out_ref[i, 0:16, :] = mean_ref[i]
        out_ref[i, 16:24, :] = total


def finish(part_ref, own_ref, side_ref, solution_ref, post_ref):
    total = part_ref[0]
    for i in range(1, NQ):
        total = total + part_ref[i]
    mean, scalars = total[0:16], total[16:17]
    s, t, rr = column(scalars, 0), column(scalars, 16), column(scalars, 32)
    own_r = own_ref[:, 0:64]
    bb, bw = own_ref[:, 64:65], own_ref[:, 65:66]
    alpha0 = bb / bw
    beta = rr / bb
    alpha1 = rr / (s + 2.0 * beta * t + beta * beta * bw)
    target = side_ref[:, 0:64]
    solution_ref[...] = alpha0 * target + alpha1 * (own_r + beta * target)
    post_ref[...] = (alpha0 + alpha1 * beta) * mean[:, :64] + alpha1 * mean[:, 64:]


def shape(*dims, dtype=F32):
    return jax.ShapeDtypeStruct(dims, dtype)


def in_hbm(array):
    return pltpu.with_memory_space_constraint(array, pltpu.HBM)


def per_device(train_points, cand_points, inv_length, noise, targets):
    def call(kernel, **options):
        return pl.pallas_call(kernel, compiler_params=PARAMS, **options)

    vmem = pl.BlockSpec(memory_space=pltpu.VMEM)
    hbm = pl.BlockSpec(memory_space=pltpu.HBM)
    build = [
        pltpu.VMEM((128, ROWS), BF16),
        pltpu.VMEM((128, ROWS), F32),
        pltpu.VMEM((128, ROWS), F32),
    ]
    build_cost = pl.CostEstimate(
        flops=2 * ROWS * COLS * 160, bytes_accessed=2 * ROWS * COLS, transcendentals=2 * ROWS * COLS
    )

    y_out, z_out, side = call(
        prepare,
        in_specs=[hbm] * 5,
        out_shape=(
            shape(80, 128, dtype=BF16),
            shape(NZ, 48, 128, dtype=BF16),
            shape(RHS, 128),
        ),
        scratch_shapes=[
            pltpu.VMEM((D, S), F32),
            pltpu.VMEM((D, S), F32),
            pltpu.VMEM((1, D), F32),
            pltpu.VMEM((1, S), F32),
            pltpu.VMEM((RHS, S), F32),
            pltpu.SemaphoreType.DMA((5,)),
        ],
    )(
        in_hbm(train_points),
        in_hbm(cand_points),
        in_hbm(inv_length.reshape(1, D)),
        in_hbm(noise.reshape(1, S)),
        in_hbm(targets),
    )
    z_in = lax.all_gather(lax.all_to_all(z_out, "z", 0, 0), "c", axis=0)
    far = lax.ppermute(y_out, "far", [(0, 1), (1, 0)])
    y_half = call(
        order,
        out_shape=shape(8, 2, 80, 128, dtype=BF16),
        cost_estimate=pl.CostEstimate(flops=0, bytes_accessed=400000, transcendentals=0),
    )(y_out, far)
    y_in = lax.all_to_all(y_half, ("near", "x"), 0, 0)
    col, b_col = call(
        col_side,
        out_shape=(shape(COLS, 128, dtype=BF16), shape(32, COLS, dtype=BF16)),
        cost_estimate=pl.CostEstimate(
            flops=COLS * 1000, bytes_accessed=4 * COLS * 128, transcendentals=0
        ),
    )(z_in)
    kern, kept, image_out = call(
        first_apply,
        out_specs=(hbm, vmem, vmem),
        out_shape=(
            pltpu.HBM((STORED * PIECE, ROWS), BF16),
            shape(KEPT * PIECE, ROWS, dtype=BF16),
            shape(NQ, RHS, ROWS, dtype=BF16),
        ),
        scratch_shapes=[
            pltpu.VMEM((RHS, ROWS), F32),
            *build,
            pltpu.VMEM((COLS, ROWS), BF16),
            pltpu.SemaphoreType.DMA((STORED,)),
        ],
        cost_estimate=build_cost,
    )(y_in, col, b_col, side)
    image_in = lax.all_to_all(image_out, ("far", "near", "x"), 0, 0)
    w_out, w_row, b_row = call(
        merge_image,
        out_shape=(shape(NZ, RHS, 128, dtype=BF16), shape(RHS, ROWS), shape(RHS, ROWS)),
    )(image_in, y_in)
    w_in = lax.all_gather(lax.all_to_all(w_out, "z", 0, 0), "c", axis=0)
    scalar_out, r_col, own = call(
        second_apply,
        in_specs=[vmem] * 4 + [hbm, vmem, vmem],
        out_shape=(shape(NZ, 1, 128), shape(32, COLS, dtype=BF16), shape(RHS, 128)),
        scratch_shapes=[
            pltpu.VMEM((STORED * PIECE, ROWS), BF16),
            pltpu.SemaphoreType.DMA((READS,)),
        ],
    )(w_in, b_col, w_row, b_row, in_hbm(kern), kept, side)
    scalar_in = lax.all_gather(lax.all_to_all(scalar_out, "z", 0, 0), "c", axis=0)
    mean_part = call(
        cand_mean,
        out_shape=shape(NQ, RHS, 128),
        scratch_shapes=[*build, *[pltpu.VMEM((COLS, ROWS), BF16)] * 2],
        cost_estimate=build_cost,
    )(y_in, col, b_col, r_col)
    mean_out = call(pack, out_shape=shape(NQ, 24, 128))(scalar_in, mean_part)
    mean_in = lax.all_to_all(mean_out, ("far", "near", "x"), 0, 0)
    return call(finish, out_shape=(shape(RHS, S), shape(RHS, S)))(mean_in, own, side)


def solution(mesh):
    fine = Mesh(mesh.devices.reshape(16, 2, 2, 2, 4), ("z", "c", "far", "near", "x"))
    every = ("z", "c", "far", "near", "x")
    wide = P(None, every)
    return jax.shard_map(
        per_device,
        mesh=fine,
        in_specs=(wide, wide, P(), P(every), wide),
        out_specs=(wide, wide),
        check_vma=False,
    )
```

```python
import math

import jax
import jax.numpy as jnp
from jax import lax
from jax.experimental import pallas as pl
from jax.experimental.pallas import tpu as pltpu
from jax.sharding import Mesh, PartitionSpec as P

F32 = jnp.float32
BF16 = jnp.bfloat16

D = 64
S = 64
RHS = 16
NQ = 16
NZ = 16
ROWS = NQ * S
COLS = 2 * NZ * S
LOG2E = math.log2(math.e)
CHUNKS = 4
PIECE = COLS // CHUNKS
KEPT = 1
STORED = CHUNKS - KEPT
READ = 512
READS = STORED * PIECE // READ
PARAMS = pltpu.CompilerParams(vmem_limit_bytes=24 * 1024 * 1024)


def halves(value):
    high = value.astype(BF16)
    return high, (value - high.astype(F32)).astype(BF16)


def thirds(value):
    high = value.astype(BF16).astype(F32)
    rest = value - high
    middle = rest.astype(BF16).astype(F32)
    low = (rest - middle).astype(BF16).astype(F32)
    return high, middle, low


def rows_of(width, pieces):
    index = lax.broadcasted_iota(jnp.int32, (16, width), 0)
    total = jnp.zeros((16, width), F32)
    for i, piece in enumerate(pieces):
        total = jnp.where(index == i, piece, total)
    return total


def column(row, start):
    lane = lax.broadcasted_iota(jnp.int32, (RHS, 128), 1)
    index = lax.broadcasted_iota(jnp.int32, (RHS, 128), 0)
    return jnp.sum(jnp.where(lane == index + start, row, 0.0), axis=1, keepdims=True)


def prepare(
    train_hbm, cand_hbm, inv_hbm, noise_hbm, target_hbm, y_ref, z_ref, side_ref,
    train_ref, cand_ref, inv_ref, noise_ref, target_ref, sems,
):
    copies = [
        pltpu.make_async_copy(source, target, sems.at[i])
        for i, (source, target) in enumerate(
            [
                (train_hbm, train_ref),
                (inv_hbm, inv_ref),
                (target_hbm, target_ref),
                (cand_hbm, cand_ref),
                (noise_hbm, noise_ref),
            ]
        )
    ]
    for copy in copies:
        copy.start()
    for copy in copies:
        copy.wait()
    eye = lax.broadcasted_iota(jnp.int32, (D, D), 0) == lax.broadcasted_iota(
        jnp.int32, (D, D), 1
    )
    inv = jnp.sum(jnp.where(eye, inv_ref[...], 0.0), axis=1, keepdims=True)
    train = train_ref[...] * inv
    cand = cand_ref[...] * inv
    target = target_ref[...]
    b_high, b_low = halves(target)
    b = jnp.concatenate([b_high, b_low], axis=1)
    both = jnp.concatenate([train.astype(BF16), cand.astype(BF16)], axis=1)
    folded = jnp.concatenate([train[:32].astype(BF16), train[32:].astype(BF16)], axis=1)
    for i in range(NZ):
        z_ref[i, 0:32, :] = folded
        z_ref[i, 32:48, :] = b
    y_ref[0:64, :] = both
    y_ref[64:80, :] = b
    side_ref[...] = jnp.concatenate(
        [target, jnp.broadcast_to(noise_ref[...], (RHS, S))], axis=1
    )


def order(own_ref, far_ref, out_ref):
    far = lax.axis_index("far")
    for k, ref in enumerate([own_ref, far_ref]):
        value = ref[...]
        for i in range(8):
            out_ref[i, (far + k) % 2] = value


def shard(ref, q, rows, lanes=slice(None)):
    y, x = q // 4, q % 4
    return ref[(y % 2) * 4 + x, y // 2, rows, lanes]


def row_side(y_ref, j, first):
    points = jnp.concatenate(
        [
            shard(y_ref, 2 * j, slice(0, 64), slice(first, first + 64)),
            shard(y_ref, 2 * j + 1, slice(0, 64), slice(first, first + 64)),
        ],
        axis=1,
    ).astype(F32)
    norm = jnp.sum(points * points, axis=0, keepdims=True)
    extra = rows_of(128, [*thirds(norm), 1.0, 1.0, 1.0])
    return jnp.concatenate(
        [-2.0 * points, extra, jnp.zeros((48, 128), F32)], axis=0
    ).astype(BF16)


def col_side(z_ref, col_ref, b_ref):
    for z in range(NZ):
        low, high = z_ref[0, z].astype(F32), z_ref[1, z].astype(F32)
        first = jnp.concatenate([low[:, :64], high[:, :64]], axis=1)
        second = jnp.concatenate([low[:, 64:], high[:, 64:]], axis=1)
        points = jnp.concatenate([first[0:32], second[0:32]], axis=0)
        b_ref[:, z * 128 : z * 128 + 128] = jnp.concatenate(
            [first[32:48], second[32:48]], axis=0
        ).astype(BF16)
        norm = jnp.sum(points * points, axis=0, keepdims=True)
        extra = rows_of(128, [1.0, 1.0, 1.0, *thirds(norm)])
        full = jnp.concatenate([points, extra, jnp.zeros((48, 128), F32)], axis=0)
        col_ref[z * 128 : z * 128 + 128, :] = full.T.astype(BF16)


def matern_of(inner):
    five_dist = jnp.maximum(inner, 1e-30) * 5.0
    scaled = five_dist * lax.rsqrt(five_dist)
    return (1.0 + scaled + five_dist * (1.0 / 3.0)) * jnp.exp2(scaled * (-LOG2E))


def piece(tile_ref, hbm_ref, sems, i):
    span = pl.ds(pl.multiple_of(i * PIECE, PIECE), PIECE)
    return tile_ref.at[span, :], hbm_ref.at[span, :], sems.at[i]


def fill(col_ref, row_ref, kern_ref, even_ref, odd_ref, before=None, low_ref=None):
    def inner(z, out_ref):
        points = col_ref[pl.ds(pl.multiple_of(z * 128, 128), 128), :]
        out_ref[...] = jnp.dot(points, row_ref[...], preferred_element_type=F32)

    def spread(z, in_ref):
        for i in range(8):
            span = pl.ds(pl.multiple_of(z * 128 + i * 16, 16), 16)
            kern = matern_of(in_ref[i * 16 : i * 16 + 16, :])
            if low_ref is None:
                kern_ref[span, :] = kern.astype(BF16)
            else:
                high, low = halves(kern)
                kern_ref[span, :] = high
                low_ref[span, :] = low

    def step(i, _):
        if before is not None:
            before(i)
        buffers = [even_ref, odd_ref]
        for k in range(4):
            z = 4 * i + k
            inner(jnp.minimum(z + 1, NZ - 1), buffers[(k + 1) % 2])
            spread(z, buffers[k % 2])
        return 0

    inner(0, even_ref)
    lax.fori_loop(0, NZ // 4, step, 0)


def own_block(q):
    return pl.ds(pl.multiple_of((q // 2) * 128, 128), 128)


def own_mask(q):
    lane = lax.broadcasted_iota(jnp.int32, (RHS, 128), 1)
    return (lane // 64) == (q % 2)


def position():
    return (lax.axis_index("far") * 2 + lax.axis_index("near")) * 4 + lax.axis_index("x")


def first_apply(
    y_ref, col_ref, b_ref, side_ref, hbm_ref, kept_ref, out_ref,
    acc_ref, row_ref, even_ref, odd_ref, kern_ref, sems,
):
    q = position()
    for j in range(NQ // 2):
        row_ref[:, j * 128 : j * 128 + 128] = row_side(y_ref, j, 0)

    def before(i):
        @pl.when(i > 0)
        def _():
            pltpu.make_async_copy(*piece(kern_ref, hbm_ref, sems, i - 1)).start()

    fill(col_ref, row_ref, kern_ref, even_ref, odd_ref, before)
    total = jnp.dot(b_ref[...], kern_ref[...], preferred_element_type=F32)
    acc_ref[...] = total[0:16] + total[16:32]
    kept_ref[...] = kern_ref[STORED * PIECE :, :]
    own = side_ref[:, 0:64] * side_ref[:, 64:128]
    twice = jnp.concatenate([own, own], axis=1)
    acc_ref[:, own_block(q)] += jnp.where(own_mask(q), twice, 0.0)
    image = acc_ref[...].astype(BF16)
    for i in range(NQ):
        out_ref[i] = image
    for i in range(STORED):
        pltpu.make_async_copy(*piece(kern_ref, hbm_ref, sems, i)).wait()


def merge_image(part_ref, y_ref, out_ref, w_ref, br_ref):
    q = position()
    total = part_ref[0].astype(F32)
    for i in range(1, NQ):
        total = total + part_ref[i].astype(F32)
    w_ref[...] = total
    for j in range(NQ // 2):
        even = shard(y_ref, 2 * j, slice(64, 80)).astype(F32)
        odd = shard(y_ref, 2 * j + 1, slice(64, 80)).astype(F32)
        br_ref[:, j * 128 : j * 128 + 128] = jnp.concatenate(
            [even[:, :64] + even[:, 64:], odd[:, :64] + odd[:, 64:]], axis=1
        )
    b = br_ref[...]
    bw = jnp.sum(b * total, axis=1, keepdims=True)
    bb = jnp.sum(b * b, axis=1, keepdims=True)
    block = w_ref[:, own_block(q)]
    own = jnp.where(q % 2 == 0, block[:, :64], block[:, 64:])
    lane = lax.broadcasted_iota(jnp.int32, (RHS, 64), 1)
    scalars = jnp.zeros((RHS, 64), F32)
    for i, piece in enumerate([*thirds(bw), *thirds(bb)]):
        scalars = jnp.where(lane == i, piece, scalars)
    message = jnp.concatenate([own, scalars], axis=1).astype(BF16)
    for i in range(NZ):
        out_ref[i] = message


def fetch(hbm_ref, tile_ref, sems, i):
    span = slice(i * READ, i * READ + READ)
    return pltpu.make_async_copy(hbm_ref.at[span, :], tile_ref.at[span, :], sems.at[i])


def streamed(r_ref, hbm_ref, tile_ref, sems, kept_ref):
    total = jnp.dot(r_ref[:, STORED * PIECE :], kept_ref[...], preferred_element_type=F32)
    for i in range(READS):
        fetch(hbm_ref, tile_ref, sems, i).wait()
        span = slice(i * READ, i * READ + READ)
        total = total + jnp.dot(r_ref[:, span], tile_ref[span, :], preferred_element_type=F32)
    return total[0:16] + total[16:32]


def second_apply(
    s_ref, b_ref, w_ref, br_ref, kern_hbm, kept_ref, side_ref, out_ref, r_ref, own_ref,
    kern_ref, sems,
):
    for i in range(READS):
        fetch(kern_hbm, kern_ref, sems, i).start()
    q = position()
    sums = s_ref[0, 0, :, 64:128].astype(F32)
    for c in range(2):
        for z in range(NZ):
            if c or z:
                sums = sums + s_ref[c, z, :, 64:128].astype(F32)
    lane = lax.broadcasted_iota(jnp.int32, (RHS, 64), 1)
    bw = jnp.sum(jnp.where(lane < 3, sums, 0.0), axis=1, keepdims=True)
    bb = jnp.sum(jnp.where((lane >= 3) & (lane < 6), sums, 0.0), axis=1, keepdims=True)
    alpha = bb / bw
    for z in range(NZ):
        span = slice(z * 128, z * 128 + 128)
        w = jnp.concatenate([s_ref[0, z, :, 0:64], s_ref[1, z, :, 0:64]], axis=1).astype(F32)
        b = b_ref[0:16, span].astype(F32) + b_ref[16:32, span].astype(F32)
        high, low = halves(b - alpha * w)
        r_ref[:, span] = jnp.concatenate([high, low], axis=0)
    r_row = br_ref[...] - alpha * w_ref[...]
    block = w_ref[:, own_block(q)]
    own_w = jnp.where(q % 2 == 0, block[:, :64], block[:, 64:])
    target, noise = side_ref[:, 0:64], side_ref[:, 64:128]
    own_r = target - alpha * own_w
    t = jnp.sum(own_r * own_w, axis=1, keepdims=True)
    rr = jnp.sum(own_r * own_r, axis=1, keepdims=True)
    side = jnp.where(lane == 0, bb, jnp.where(lane == 1, bw, 0.0))
    own_ref[...] = jnp.concatenate([own_r, side], axis=1)
    applied = streamed(r_ref, kern_hbm, kern_ref, sems, kept_ref)
    s = jnp.sum(r_row * applied, axis=1, keepdims=True) + jnp.sum(
        noise * own_r * own_r, axis=1, keepdims=True
    )
    wide = lax.broadcasted_iota(jnp.int32, (RHS, 128), 1)
    index = lax.broadcasted_iota(jnp.int32, (RHS, 128), 0)
    spread = (
        jnp.where(wide == index, s, 0.0)
        + jnp.where(wide == index + 16, t, 0.0)
        + jnp.where(wide == index + 32, rr, 0.0)
    )
    spread = jnp.sum(spread, axis=0, keepdims=True)
    for i in range(NZ):
        out_ref[i] = spread


def cand_mean(
    y_ref, col_ref, b_ref, r_ref, out_ref, row_ref, even_ref, odd_ref, kern_ref, low_ref
):
    for j in range(NQ // 2):
        row_ref[:, j * 128 : j * 128 + 128] = row_side(y_ref, j, 64)
    fill(col_ref, row_ref, kern_ref, even_ref, odd_ref, low_ref=low_ref)
    vectors = jnp.concatenate([b_ref[...], r_ref[...]], axis=0)
    total = jnp.dot(vectors, kern_ref[...], preferred_element_type=F32) + jnp.dot(
        vectors, low_ref[...], preferred_element_type=F32
    )
    mean0, mean = total[0:16] + total[16:32], total[32:48] + total[48:64]
    for i in range(NQ):
        span = slice(i * 64, i * 64 + 64)
        out_ref[i] = jnp.concatenate([mean0[:, span], mean[:, span]], axis=1)


def pack(s_ref, mean_ref, out_ref):
    total = s_ref[0, 0]
    for c in range(2):
        for z in range(NZ):
            if c or z:
                total = total + s_ref[c, z]
    eight = lax.broadcasted_iota(jnp.int32, (8, 128), 0)
    total = jnp.where(eight == 0, total, 0.0)
    for i in range(NQ):
        out_ref[i, 0:16, :] = mean_ref[i]
        out_ref[i, 16:24, :] = total


def finish(part_ref, own_ref, side_ref, solution_ref, post_ref):
    total = part_ref[0]
    for i in range(1, NQ):
        total = total + part_ref[i]
    mean, scalars = total[0:16], total[16:17]
    s, t, rr = column(scalars, 0), column(scalars, 16), column(scalars, 32)
    own_r = own_ref[:, 0:64]
    bb, bw = own_ref[:, 64:65], own_ref[:, 65:66]
    alpha0 = bb / bw
    beta = rr / bb
    alpha1 = rr / (s + 2.0 * beta * t + beta * beta * bw)
    target = side_ref[:, 0:64]
    solution_ref[...] = alpha0 * target + alpha1 * (own_r + beta * target)
    post_ref[...] = (alpha0 + alpha1 * beta) * mean[:, :64] + alpha1 * mean[:, 64:]


def shape(*dims, dtype=F32):
    return jax.ShapeDtypeStruct(dims, dtype)


def in_hbm(array):
    return pltpu.with_memory_space_constraint(array, pltpu.HBM)


def per_device(train_points, cand_points, inv_length, noise, targets):
    def call(kernel, **options):
        return pl.pallas_call(kernel, compiler_params=PARAMS, **options)

    vmem = pl.BlockSpec(memory_space=pltpu.VMEM)
    hbm = pl.BlockSpec(memory_space=pltpu.HBM)
    build = [
        pltpu.VMEM((128, ROWS), BF16),
        pltpu.VMEM((128, ROWS), F32),
        pltpu.VMEM((128, ROWS), F32),
    ]
    build_cost = pl.CostEstimate(
        flops=2 * ROWS * COLS * 160, bytes_accessed=2 * ROWS * COLS, transcendentals=2 * ROWS * COLS
    )

    y_out, z_out, side = call(
        prepare,
        in_specs=[hbm] * 5,
        out_shape=(
            shape(80, 128, dtype=BF16),
            shape(NZ, 48, 128, dtype=BF16),
            shape(RHS, 128),
        ),
        scratch_shapes=[
            pltpu.VMEM((D, S), F32),
            pltpu.VMEM((D, S), F32),
            pltpu.VMEM((1, D), F32),
            pltpu.VMEM((1, S), F32),
            pltpu.VMEM((RHS, S), F32),
            pltpu.SemaphoreType.DMA((5,)),
        ],
    )(
        in_hbm(train_points),
        in_hbm(cand_points),
        in_hbm(inv_length.reshape(1, D)),
        in_hbm(noise.reshape(1, S)),
        in_hbm(targets),
    )
    z_in = lax.all_gather(lax.all_to_all(z_out, "z", 0, 0), "c", axis=0)
    far = lax.ppermute(y_out, "far", [(0, 1), (1, 0)])
    y_half = call(
        order,
        out_shape=shape(8, 2, 80, 128, dtype=BF16),
        cost_estimate=pl.CostEstimate(flops=0, bytes_accessed=400000, transcendentals=0),
    )(y_out, far)
    y_in = lax.all_to_all(y_half, ("near", "x"), 0, 0)
    col, b_col = call(
        col_side,
        out_shape=(shape(COLS, 128, dtype=BF16), shape(32, COLS, dtype=BF16)),
        cost_estimate=pl.CostEstimate(
            flops=COLS * 1000, bytes_accessed=4 * COLS * 128, transcendentals=0
        ),
    )(z_in)
    kern, kept, image_out = call(
        first_apply,
        out_specs=(hbm, vmem, vmem),
        out_shape=(
            pltpu.HBM((STORED * PIECE, ROWS), BF16),
            shape(KEPT * PIECE, ROWS, dtype=BF16),
            shape(NQ, RHS, ROWS, dtype=BF16),
        ),
        scratch_shapes=[
            pltpu.VMEM((RHS, ROWS), F32),
            *build,
            pltpu.VMEM((COLS, ROWS), BF16),
            pltpu.SemaphoreType.DMA((STORED,)),
        ],
        cost_estimate=build_cost,
    )(y_in, col, b_col, side)
    image_in = lax.all_to_all(image_out, ("far", "near", "x"), 0, 0)
    w_out, w_row, b_row = call(
        merge_image,
        out_shape=(shape(NZ, RHS, 128, dtype=BF16), shape(RHS, ROWS), shape(RHS, ROWS)),
    )(image_in, y_in)
    w_in = lax.all_gather(lax.all_to_all(w_out, "z", 0, 0), "c", axis=0)
    scalar_out, r_col, own = call(
        second_apply,
        in_specs=[vmem] * 4 + [hbm, vmem, vmem],
        out_shape=(shape(NZ, 1, 128), shape(32, COLS, dtype=BF16), shape(RHS, 128)),
        scratch_shapes=[
            pltpu.VMEM((STORED * PIECE, ROWS), BF16),
            pltpu.SemaphoreType.DMA((READS,)),
        ],
    )(w_in, b_col, w_row, b_row, in_hbm(kern), kept, side)
    scalar_in = lax.all_gather(lax.all_to_all(scalar_out, "z", 0, 0), "c", axis=0)
    mean_part = call(
        cand_mean,
        out_shape=shape(NQ, RHS, 128),
        scratch_shapes=[*build, *[pltpu.VMEM((COLS, ROWS), BF16)] * 2],
        cost_estimate=build_cost,
    )(y_in, col, b_col, r_col)
    mean_out = call(pack, out_shape=shape(NQ, 24, 128))(scalar_in, mean_part)
    mean_in = lax.all_to_all(mean_out, ("far", "near", "x"), 0, 0)
    return call(finish, out_shape=(shape(RHS, S), shape(RHS, S)))(mean_in, own, side)


def solution(mesh):
    fine = Mesh(mesh.devices.reshape(16, 2, 2, 2, 4), ("z", "c", "far", "near", "x"))
    every = ("z", "c", "far", "near", "x")
    wide = P(None, every)
    return jax.shard_map(
        per_device,
        mesh=fine,
        in_specs=(wide, wide, P(), P(every), wide),
        out_specs=(wide, wide),
        check_vma=False,
    )
```

```python
import math

import jax
import jax.numpy as jnp
from jax import lax
from jax.experimental import pallas as pl
from jax.experimental.pallas import tpu as pltpu
from jax.sharding import Mesh, PartitionSpec as P

F32 = jnp.float32
BF16 = jnp.bfloat16

D = 64
S = 64
RHS = 16
NQ = 16
NZ = 16
ROWS = NQ * S
COLS = 2 * NZ * S
LOG2E = math.log2(math.e)
CHUNKS = 4
PIECE = COLS // CHUNKS
KEPT = 1
STORED = CHUNKS - KEPT
READ = 512
READS = STORED * PIECE // READ
PARAMS = pltpu.CompilerParams(vmem_limit_bytes=24 * 1024 * 1024)


def halves(value):
    high = value.astype(BF16)
    return high, (value - high.astype(F32)).astype(BF16)


def thirds(value):
    high = value.astype(BF16).astype(F32)
    rest = value - high
    middle = rest.astype(BF16).astype(F32)
    low = (rest - middle).astype(BF16).astype(F32)
    return high, middle, low


def rows_of(width, pieces):
    index = lax.broadcasted_iota(jnp.int32, (16, width), 0)
    total = jnp.zeros((16, width), F32)
    for i, piece in enumerate(pieces):
        total = jnp.where(index == i, piece, total)
    return total


def column(row, start):
    lane = lax.broadcasted_iota(jnp.int32, (RHS, 128), 1)
    index = lax.broadcasted_iota(jnp.int32, (RHS, 128), 0)
    return jnp.sum(jnp.where(lane == index + start, row, 0.0), axis=1, keepdims=True)


def prepare(
    train_hbm, cand_hbm, inv_hbm, noise_hbm, target_hbm, y_ref, z_ref, side_ref,
    train_ref, cand_ref, inv_ref, noise_ref, target_ref, sems,
):
    copies = [
        pltpu.make_async_copy(source, target, sems.at[i])
        for i, (source, target) in enumerate(
            [
                (train_hbm, train_ref),
                (inv_hbm, inv_ref),
                (target_hbm, target_ref),
                (cand_hbm, cand_ref),
                (noise_hbm, noise_ref),
            ]
        )
    ]
    for copy in copies:
        copy.start()
    for copy in copies[:3]:
        copy.wait()
    eye = lax.broadcasted_iota(jnp.int32, (D, D), 0) == lax.broadcasted_iota(
        jnp.int32, (D, D), 1
    )
    inv = jnp.sum(jnp.where(eye, inv_ref[...], 0.0), axis=1, keepdims=True)
    train = train_ref[...] * inv
    target = target_ref[...]
    b_high, b_low = halves(target)
    b = jnp.concatenate([b_high, b_low], axis=1)
    folded = jnp.concatenate([train[:32].astype(BF16), train[32:].astype(BF16)], axis=1)
    for i in range(NZ):
        z_ref[i, 0:32, :] = folded
        z_ref[i, 32:48, :] = b
    for copy in copies[3:]:
        copy.wait()
    cand = cand_ref[...] * inv
    both = jnp.concatenate([train.astype(BF16), cand.astype(BF16)], axis=1)
    y_ref[0:64, :] = both
    y_ref[64:80, :] = b
    side_ref[...] = jnp.concatenate(
        [target, jnp.broadcast_to(noise_ref[...], (RHS, S))], axis=1
    )


def order(own_ref, far_ref, out_ref):
    far = lax.axis_index("far")
    for k, ref in enumerate([own_ref, far_ref]):
        value = ref[...]
        for i in range(8):
            out_ref[i, (far + k) % 2] = value


def shard(ref, q, rows, lanes=slice(None)):
    y, x = q // 4, q % 4
    return ref[(y % 2) * 4 + x, y // 2, rows, lanes]


def row_side(y_ref, j, first):
    points = jnp.concatenate(
        [
            shard(y_ref, 2 * j, slice(0, 64), slice(first, first + 64)),
            shard(y_ref, 2 * j + 1, slice(0, 64), slice(first, first + 64)),
        ],
        axis=1,
    ).astype(F32)
    norm = jnp.sum(points * points, axis=0, keepdims=True)
    extra = rows_of(128, [*thirds(norm), 1.0, 1.0, 1.0])
    return jnp.concatenate(
        [-2.0 * points, extra, jnp.zeros((48, 128), F32)], axis=0
    ).astype(BF16)


def col_side(z_ref, col_ref, b_ref):
    for z in range(NZ):
        low, high = z_ref[0, z].astype(F32), z_ref[1, z].astype(F32)
        first = jnp.concatenate([low[:, :64], high[:, :64]], axis=1)
        second = jnp.concatenate([low[:, 64:], high[:, 64:]], axis=1)
        points = jnp.concatenate([first[0:32], second[0:32]], axis=0)
        b_ref[:, z * 128 : z * 128 + 128] = jnp.concatenate(
            [first[32:48], second[32:48]], axis=0
        ).astype(BF16)
        norm = jnp.sum(points * points, axis=0, keepdims=True)
        extra = rows_of(128, [1.0, 1.0, 1.0, *thirds(norm)])
        full = jnp.concatenate([points, extra, jnp.zeros((48, 128), F32)], axis=0)
        col_ref[z * 128 : z * 128 + 128, :] = full.T.astype(BF16)


def matern_of(inner):
    five_dist = jnp.maximum(inner, 1e-30) * 5.0
    scaled = five_dist * lax.rsqrt(five_dist)
    return (1.0 + scaled + five_dist * (1.0 / 3.0)) * jnp.exp2(scaled * (-LOG2E))


def piece(tile_ref, hbm_ref, sems, i):
    span = pl.ds(pl.multiple_of(i * PIECE, PIECE), PIECE)
    return tile_ref.at[span, :], hbm_ref.at[span, :], sems.at[i]


def fill(col_ref, row_ref, kern_ref, even_ref, odd_ref, before=None, low_ref=None):
    def inner(z, out_ref):
        points = col_ref[pl.ds(pl.multiple_of(z * 128, 128), 128), :]
        out_ref[...] = jnp.dot(points, row_ref[...], preferred_element_type=F32)

    def spread(z, in_ref):
        for i in range(8):
            span = pl.ds(pl.multiple_of(z * 128 + i * 16, 16), 16)
            kern = matern_of(in_ref[i * 16 : i * 16 + 16, :])
            if low_ref is None:
                kern_ref[span, :] = kern.astype(BF16)
            else:
                high, low = halves(kern)
                kern_ref[span, :] = high
                low_ref[span, :] = low

    def step(i, _):
        if before is not None:
            before(i)
        buffers = [even_ref, odd_ref]
        for k in range(4):
            z = 4 * i + k
            inner(jnp.minimum(z + 1, NZ - 1), buffers[(k + 1) % 2])
            spread(z, buffers[k % 2])
        return 0

    inner(0, even_ref)
    lax.fori_loop(0, NZ // 4, step, 0)


def own_block(q):
    return pl.ds(pl.multiple_of((q // 2) * 128, 128), 128)


def own_mask(q):
    lane = lax.broadcasted_iota(jnp.int32, (RHS, 128), 1)
    return (lane // 64) == (q % 2)


def position():
    return (lax.axis_index("far") * 2 + lax.axis_index("near")) * 4 + lax.axis_index("x")


def first_apply(
    y_ref, col_ref, b_ref, side_ref, hbm_ref, kept_ref, out_ref,
    acc_ref, row_ref, even_ref, odd_ref, kern_ref, sems,
):
    q = position()
    for j in range(NQ // 2):
        row_ref[:, j * 128 : j * 128 + 128] = row_side(y_ref, j, 0)

    def before(i):
        @pl.when(i > 0)
        def _():
            pltpu.make_async_copy(*piece(kern_ref, hbm_ref, sems, i - 1)).start()

    fill(col_ref, row_ref, kern_ref, even_ref, odd_ref, before)
    total = jnp.dot(b_ref[...], kern_ref[...], preferred_element_type=F32)
    acc_ref[...] = total[0:16] + total[16:32]
    kept_ref[...] = kern_ref[STORED * PIECE :, :]
    own = side_ref[:, 0:64] * side_ref[:, 64:128]
    twice = jnp.concatenate([own, own], axis=1)
    acc_ref[:, own_block(q)] += jnp.where(own_mask(q), twice, 0.0)
    image = acc_ref[...].astype(BF16)
    for i in range(NQ):
        out_ref[i] = image
    for i in range(STORED):
        pltpu.make_async_copy(*piece(kern_ref, hbm_ref, sems, i)).wait()


def merge_image(part_ref, y_ref, out_ref, w_ref, br_ref):
    q = position()
    total = part_ref[0].astype(F32)
    for i in range(1, NQ):
        total = total + part_ref[i].astype(F32)
    w_ref[...] = total
    for j in range(NQ // 2):
        even = shard(y_ref, 2 * j, slice(64, 80)).astype(F32)
        odd = shard(y_ref, 2 * j + 1, slice(64, 80)).astype(F32)
        br_ref[:, j * 128 : j * 128 + 128] = jnp.concatenate(
            [even[:, :64] + even[:, 64:], odd[:, :64] + odd[:, 64:]], axis=1
        )
    b = br_ref[...]
    bw = jnp.sum(b * total, axis=1, keepdims=True)
    bb = jnp.sum(b * b, axis=1, keepdims=True)
    block = w_ref[:, own_block(q)]
    own = jnp.where(q % 2 == 0, block[:, :64], block[:, 64:])
    lane = lax.broadcasted_iota(jnp.int32, (RHS, 64), 1)
    scalars = jnp.zeros((RHS, 64), F32)
    for i, piece in enumerate([*thirds(bw), *thirds(bb)]):
        scalars = jnp.where(lane == i, piece, scalars)
    message = jnp.concatenate([own, scalars], axis=1).astype(BF16)
    for i in range(NZ):
        out_ref[i] = message


def fetch(hbm_ref, tile_ref, sems, i):
    span = slice(i * READ, i * READ + READ)
    return pltpu.make_async_copy(hbm_ref.at[span, :], tile_ref.at[span, :], sems.at[i])


def streamed(r_ref, hbm_ref, tile_ref, sems, kept_ref):
    total = jnp.dot(r_ref[:, STORED * PIECE :], kept_ref[...], preferred_element_type=F32)
    for i in range(READS):
        fetch(hbm_ref, tile_ref, sems, i).wait()
        span = slice(i * READ, i * READ + READ)
        total = total + jnp.dot(r_ref[:, span], tile_ref[span, :], preferred_element_type=F32)
    return total[0:16] + total[16:32]


def second_apply(
    s_ref, b_ref, w_ref, br_ref, kern_hbm, kept_ref, side_ref, out_ref, r_ref, own_ref,
    kern_ref, sems,
):
    for i in range(READS):
        fetch(kern_hbm, kern_ref, sems, i).start()
    q = position()
    sums = s_ref[0, 0, :, 64:128].astype(F32)
    for c in range(2):
        for z in range(NZ):
            if c or z:
                sums = sums + s_ref[c, z, :, 64:128].astype(F32)
    lane = lax.broadcasted_iota(jnp.int32, (RHS, 64), 1)
    bw = jnp.sum(jnp.where(lane < 3, sums, 0.0), axis=1, keepdims=True)
    bb = jnp.sum(jnp.where((lane >= 3) & (lane < 6), sums, 0.0), axis=1, keepdims=True)
    alpha = bb / bw
    for z in range(NZ):
        span = slice(z * 128, z * 128 + 128)
        w = jnp.concatenate([s_ref[0, z, :, 0:64], s_ref[1, z, :, 0:64]], axis=1).astype(F32)
        b = b_ref[0:16, span].astype(F32) + b_ref[16:32, span].astype(F32)
        high, low = halves(b - alpha * w)
        r_ref[:, span] = jnp.concatenate([high, low], axis=0)
    r_row = br_ref[...] - alpha * w_ref[...]
    block = w_ref[:, own_block(q)]
    own_w = jnp.where(q % 2 == 0, block[:, :64], block[:, 64:])
    target, noise = side_ref[:, 0:64], side_ref[:, 64:128]
    own_r = target - alpha * own_w
    t = jnp.sum(own_r * own_w, axis=1, keepdims=True)
    rr = jnp.sum(own_r * own_r, axis=1, keepdims=True)
    side = jnp.where(lane == 0, bb, jnp.where(lane == 1, bw, 0.0))
    own_ref[...] = jnp.concatenate([own_r, side], axis=1)
    applied = streamed(r_ref, kern_hbm, kern_ref, sems, kept_ref)
    s = jnp.sum(r_row * applied, axis=1, keepdims=True) + jnp.sum(
        noise * own_r * own_r, axis=1, keepdims=True
    )
    wide = lax.broadcasted_iota(jnp.int32, (RHS, 128), 1)
    index = lax.broadcasted_iota(jnp.int32, (RHS, 128), 0)
    spread = (
        jnp.where(wide == index, s, 0.0)
        + jnp.where(wide == index + 16, t, 0.0)
        + jnp.where(wide == index + 32, rr, 0.0)
    )
    spread = jnp.sum(spread, axis=0, keepdims=True)
    for i in range(NZ):
        out_ref[i] = spread


def cand_mean(
    y_ref, col_ref, b_ref, r_ref, out_ref, row_ref, even_ref, odd_ref, kern_ref, low_ref
):
    for j in range(NQ // 2):
        row_ref[:, j * 128 : j * 128 + 128] = row_side(y_ref, j, 64)
    fill(col_ref, row_ref, kern_ref, even_ref, odd_ref, low_ref=low_ref)
    vectors = jnp.concatenate([b_ref[...], r_ref[...]], axis=0)
    total = jnp.dot(vectors, kern_ref[...], preferred_element_type=F32) + jnp.dot(
        vectors, low_ref[...], preferred_element_type=F32
    )
    mean0, mean = total[0:16] + total[16:32], total[32:48] + total[48:64]
    for i in range(NQ):
        span = slice(i * 64, i * 64 + 64)
        out_ref[i] = jnp.concatenate([mean0[:, span], mean[:, span]], axis=1)


def pack(s_ref, mean_ref, out_ref):
    total = s_ref[0, 0]
    for c in range(2):
        for z in range(NZ):
            if c or z:
                total = total + s_ref[c, z]
    eight = lax.broadcasted_iota(jnp.int32, (8, 128), 0)
    total = jnp.where(eight == 0, total, 0.0)
    for i in range(NQ):
        out_ref[i, 0:16, :] = mean_ref[i]
        out_ref[i, 16:24, :] = total


def finish(part_ref, own_ref, side_ref, solution_ref, post_ref):
    total = part_ref[0]
    for i in range(1, NQ):
        total = total + part_ref[i]
    mean, scalars = total[0:16], total[16:17]
    s, t, rr = column(scalars, 0), column(scalars, 16), column(scalars, 32)
    own_r = own_ref[:, 0:64]
    bb, bw = own_ref[:, 64:65], own_ref[:, 65:66]
    alpha0 = bb / bw
    beta = rr / bb
    alpha1 = rr / (s + 2.0 * beta * t + beta * beta * bw)
    target = side_ref[:, 0:64]
    solution_ref[...] = alpha0 * target + alpha1 * (own_r + beta * target)
    post_ref[...] = (alpha0 + alpha1 * beta) * mean[:, :64] + alpha1 * mean[:, 64:]


def shape(*dims, dtype=F32):
    return jax.ShapeDtypeStruct(dims, dtype)


def in_hbm(array):
    return pltpu.with_memory_space_constraint(array, pltpu.HBM)


def per_device(train_points, cand_points, inv_length, noise, targets):
    def call(kernel, **options):
        return pl.pallas_call(kernel, compiler_params=PARAMS, **options)

    vmem = pl.BlockSpec(memory_space=pltpu.VMEM)
    hbm = pl.BlockSpec(memory_space=pltpu.HBM)
    build = [
        pltpu.VMEM((128, ROWS), BF16),
        pltpu.VMEM((128, ROWS), F32),
        pltpu.VMEM((128, ROWS), F32),
    ]
    build_cost = pl.CostEstimate(
        flops=2 * ROWS * COLS * 160, bytes_accessed=2 * ROWS * COLS, transcendentals=2 * ROWS * COLS
    )

    y_out, z_out, side = call(
        prepare,
        in_specs=[hbm] * 5,
        out_shape=(
            shape(80, 128, dtype=BF16),
            shape(NZ, 48, 128, dtype=BF16),
            shape(RHS, 128),
        ),
        scratch_shapes=[
            pltpu.VMEM((D, S), F32),
            pltpu.VMEM((D, S), F32),
            pltpu.VMEM((1, D), F32),
            pltpu.VMEM((1, S), F32),
            pltpu.VMEM((RHS, S), F32),
            pltpu.SemaphoreType.DMA((5,)),
        ],
    )(
        in_hbm(train_points),
        in_hbm(cand_points),
        in_hbm(inv_length.reshape(1, D)),
        in_hbm(noise.reshape(1, S)),
        in_hbm(targets),
    )
    z_in = lax.all_gather(lax.all_to_all(z_out, "z", 0, 0), "c", axis=0)
    far = lax.ppermute(y_out, "far", [(0, 1), (1, 0)])
    y_half = call(
        order,
        out_shape=shape(8, 2, 80, 128, dtype=BF16),
        cost_estimate=pl.CostEstimate(flops=0, bytes_accessed=400000, transcendentals=0),
    )(y_out, far)
    y_in = lax.all_to_all(y_half, ("near", "x"), 0, 0)
    col, b_col = call(
        col_side,
        out_shape=(shape(COLS, 128, dtype=BF16), shape(32, COLS, dtype=BF16)),
        cost_estimate=pl.CostEstimate(
            flops=COLS * 1000, bytes_accessed=4 * COLS * 128, transcendentals=0
        ),
    )(z_in)
    kern, kept, image_out = call(
        first_apply,
        out_specs=(hbm, vmem, vmem),
        out_shape=(
            pltpu.HBM((STORED * PIECE, ROWS), BF16),
            shape(KEPT * PIECE, ROWS, dtype=BF16),
            shape(NQ, RHS, ROWS, dtype=BF16),
        ),
        scratch_shapes=[
            pltpu.VMEM((RHS, ROWS), F32),
            *build,
            pltpu.VMEM((COLS, ROWS), BF16),
            pltpu.SemaphoreType.DMA((STORED,)),
        ],
        cost_estimate=build_cost,
    )(y_in, col, b_col, side)
    image_in = lax.all_to_all(image_out, ("far", "near", "x"), 0, 0)
    w_out, w_row, b_row = call(
        merge_image,
        out_shape=(shape(NZ, RHS, 128, dtype=BF16), shape(RHS, ROWS), shape(RHS, ROWS)),
    )(image_in, y_in)
    w_in = lax.all_gather(lax.all_to_all(w_out, "z", 0, 0), "c", axis=0)
    scalar_out, r_col, own = call(
        second_apply,
        in_specs=[vmem] * 4 + [hbm, vmem, vmem],
        out_shape=(shape(NZ, 1, 128), shape(32, COLS, dtype=BF16), shape(RHS, 128)),
        scratch_shapes=[
            pltpu.VMEM((STORED * PIECE, ROWS), BF16),
            pltpu.SemaphoreType.DMA((READS,)),
        ],
    )(w_in, b_col, w_row, b_row, in_hbm(kern), kept, side)
    scalar_in = lax.all_gather(lax.all_to_all(scalar_out, "z", 0, 0), "c", axis=0)
    mean_part = call(
        cand_mean,
        out_shape=shape(NQ, RHS, 128),
        scratch_shapes=[*build, *[pltpu.VMEM((COLS, ROWS), BF16)] * 2],
        cost_estimate=build_cost,
    )(y_in, col, b_col, r_col)
    mean_out = call(pack, out_shape=shape(NQ, 24, 128))(scalar_in, mean_part)
    mean_in = lax.all_to_all(mean_out, ("far", "near", "x"), 0, 0)
    return call(finish, out_shape=(shape(RHS, S), shape(RHS, S)))(mean_in, own, side)


def solution(mesh):
    fine = Mesh(mesh.devices.reshape(16, 2, 2, 2, 4), ("z", "c", "far", "near", "x"))
    every = ("z", "c", "far", "near", "x")
    wide = P(None, every)
    return jax.shard_map(
        per_device,
        mesh=fine,
        in_specs=(wide, wide, P(), P(every), wide),
        out_specs=(wide, wide),
        check_vma=False,
    )
```
